32 devices in a mesh: dp: 8 (over z, x), tensor: 4 (over y, core).
Axes of the slice: x: 2, y: 2, z: 4, core: 2. Of those that a mesh axis runs over, the one named last changes fastest.
Arguments:
- block_input: float32 [8192, 1536], P(('dp', 'tensor')), may hold values from -6 to 6
- cotangent: float32 [8192, 1536], P(('dp', 'tensor')), may hold values from -6 to 6
- norm_gain: float32 [1536], replicated, may hold values from 0.5 to 1.5
- gate_proj: bfloat16 [1536, 3072], P('dp', 'tensor'), may hold values from -0.15625 to 0.15625
- value_proj: bfloat16 [1536, 3072], P('dp', 'tensor'), may hold values from -0.15625 to 0.15625
- state_proj: bfloat16 [1536, 256], P('dp'), may hold values from -0.15625 to 0.15625
- step_proj: bfloat16 [1536, 48], P('dp', 'tensor'), may hold values from -0.15625 to 0.15625
- value_conv: float32 [4, 3072], P(None, 'tensor'), may hold values from -3 to 3
- value_conv_bias: float32 [3072], P('tensor'), may hold values from -3 to 3
- state_conv: float32 [4, 256], replicated, may hold values from -3 to 3
- state_conv_bias: float32 [256], replicated, may hold values from -3 to 3
- step_bias: float32 [48], P('tensor'), may hold values from -7 to -2.3
- decay_log: float32 [48], P('tensor'), may hold values from 0 to 2.77
- skip_gain: float32 [48], P('tensor'), may hold values from 0.5 to 2
- mixer_gain: float32 [3072], P('tensor'), may hold values from 0.5 to 1.5
- out_proj: bfloat16 [3072, 1536], P('tensor', 'dp'), may hold values from -0.109375 to 0.109375
Outputs:
- block_output: float32 [8192, 1536], P(('dp', 'tensor'))
- input_grad: float32 [8192, 1536], P(('dp', 'tensor'))
- norm_gain_grad: float32 [1536], replicated
- gate_proj_grad: float32 [1536, 3072], P('dp', 'tensor')
- value_proj_grad: float32 [1536, 3072], P('dp', 'tensor')
- state_proj_grad: float32 [1536, 256], P('dp')
- step_proj_grad: float32 [1536, 48], P('dp', 'tensor')
- value_conv_grad: float32 [4, 3072], P(None, 'tensor')
- value_conv_bias_grad: float32 [3072], P('tensor')
- state_conv_grad: float32 [4, 256], replicated
- state_conv_bias_grad: float32 [256], replicated
- step_bias_grad: float32 [48], P('tensor')
- decay_log_grad: float32 [48], P('tensor')
- skip_gain_grad: float32 [48], P('tensor')
- mixer_gain_grad: float32 [3072], P('tensor')
- out_proj_grad: float32 [3072, 1536], P('tensor', 'dp')
The draws below stay inside these ranges and needn't reach their ends.
All inputs are finite; a program needn't handle non-finite values.
Results may differ from the reference program's by a relative error of at most 0.0088.
Values may be sent and summed in bfloat16 or wider, within the bound.
No kernel may reach another device: no remote copies, remote signals or barrier semaphores. Data moves between devices by JAX's collectives and lax.ppermute only.
A program may use at most 192 MiB of HBM per device.

```python
import jax
import jax.numpy as jnp
from jax import lax

D = 1536
INNER = 3072
HEADS = 48
HEADDIM = 64
NSTATE = 128
KCONV = 4
BLOCK_LEN = 256
SEQLEN = 1024
TOKENS = 8192


def with_spikes(array, own_key, source, target, shards_of, factor):
    def block_of(axis_at):
        return (jnp.arange(array.shape[axis_at]) // (array.shape[axis_at] // shards_of)).reshape((-1,) + (1,) * (array.ndim - 1 - axis_at))

    one_side = jax.random.permutation(own_key, shards_of)[block_of(target)]
    second = (block_of(target) + shards_of // 2) % shards_of
    return jnp.where((block_of(source) == one_side) | (block_of(source) == second), factor * array, array)


def block_levels(rng, dims, cuts, low, largest):
    factor_of = 1.0
    for dim, shards_of in cuts:
        heights = jax.random.uniform(jax.random.fold_in(jax.random.fold_in(rng, 6), dim), (shards_of,), jnp.float32, low / len(cuts), largest / len(cuts))
        factor_of = factor_of * jnp.repeat(jnp.exp(heights), dims[dim] // shards_of).reshape((-1,) + (1,) * (len(dims) - 1 - dim))
    return factor_of


def bell_draw(key, extent, width, limit, shards=(), dtype=jnp.bfloat16):
    loudness = block_levels(key, extent, shards, -0.22, 0.18) if shards else 1.0
    drawn = jax.random.normal(key, extent, jnp.float32) * width * loudness
    return jnp.minimum(jnp.maximum(drawn, -limit), limit).astype(dtype)


def heavy_noise(key, shape, spread, limit, shards, heavy, kind=jnp.bfloat16):
    values = spread * jax.random.normal(key, shape, jnp.float32)
    if shards:
        values = values * block_levels(key, shape, shards, -0.22, 0.18)
    return jnp.clip(with_spikes(values, jax.random.fold_in(key, 3), *heavy), -limit, limit).astype(kind)


def setup_inputs(seed: int = 0) -> dict:
    arg_keys = jax.random.split(jax.random.key(seed), 17)
    return {
        "block_input": heavy_noise(arg_keys[0], (TOKENS, D), 1.0, 6.0, ((0, 32),), (0, 1, 32, 2.75), jnp.float32),
        "cotangent": heavy_noise(arg_keys[1], (TOKENS, D), 1.0, 6.0, ((0, 32),), (0, 1, 32, 2.75), jnp.float32),
        "norm_gain": jnp.clip(1.0 + 0.1 * jax.random.normal(arg_keys[2], (D,), jnp.float32), 0.5, 1.5),
        "gate_proj": bell_draw(arg_keys[3], (D, INNER), D ** -0.5, 0.15625, ((0, 8), (1, 4))),
        "value_proj": bell_draw(arg_keys[4], (D, INNER), D ** -0.5, 0.15625, ((0, 8), (1, 4))),
        "state_proj": bell_draw(arg_keys[5], (D, 2 * NSTATE), D ** -0.5, 0.15625, ((0, 8),)),
        "step_proj": bell_draw(arg_keys[6], (D, HEADS), D ** -0.5, 0.15625, ((0, 8), (1, 4))),
        "value_conv": bell_draw(arg_keys[7], (KCONV, INNER), KCONV ** -0.5, 3.0, ((1, 4),), jnp.float32),
        "value_conv_bias": bell_draw(arg_keys[8], (INNER,), 0.5, 3.0, ((0, 4),), jnp.float32),
        "state_conv": bell_draw(arg_keys[9], (KCONV, 2 * NSTATE), KCONV ** -0.5, 3.0, (), jnp.float32),
        "state_conv_bias": bell_draw(arg_keys[10], (2 * NSTATE,), 0.5, 3.0, (), jnp.float32),
        "step_bias": jnp.clip(-7.0 + 4.7 * jax.random.uniform(arg_keys[11], (HEADS,), jnp.float32) ** block_levels(arg_keys[11], (HEADS,), ((0, 4),), -0.2, 0.2), -7.0, -2.3),
        "decay_log": jnp.clip(2.77 * jax.random.uniform(arg_keys[12], (HEADS,), jnp.float32) ** block_levels(arg_keys[12], (HEADS,), ((0, 4),), -0.2, 0.2), 0.0, 2.77),
        "skip_gain": jnp.clip(0.5 + 1.5 * jax.random.uniform(arg_keys[13], (HEADS,), jnp.float32) ** block_levels(arg_keys[13], (HEADS,), ((0, 4),), -0.2, 0.2), 0.5, 2.0),
        "mixer_gain": jnp.clip(1.0 + 0.1 * jax.random.normal(arg_keys[14], (INNER,), jnp.float32), 0.5, 1.5),
        "out_proj": bell_draw(arg_keys[15], (INNER, D), INNER ** -0.5, 0.109375, ((0, 4), (1, 8))),
    }


norm_eps = 1e-05
highest = lax.Precision.HIGHEST

def causal_conv(values, kernel, offset_bias, seq_len):
    rows_all, channels = values.shape
    seq_count = rows_all // seq_len
    taps_count = kernel.shape[0]
    shaped = values.reshape(seq_count, seq_len, channels)
    padded = jnp.pad(shaped, ((0, 0), (taps_count - 1, 0), (0, 0)))
    running = jnp.zeros_like(shaped) + offset_bias
    for offset in range(taps_count):
        running = running + padded[:, offset:offset + seq_len, :] * kernel[offset]
    return running.reshape(rows_all, channels)

def block_scan(inputs, b_rows, c_rows, steps_dt, rate, skip_term, seq_len, block_len):
    rows_all, heads_here, head_dim = inputs.shape
    state_dim = b_rows.shape[1]
    seq_count = rows_all // seq_len
    block_count = seq_len // block_len
    x_blocks = inputs.reshape(seq_count, block_count, block_len, heads_here, head_dim)
    b_blocks = b_rows.reshape(seq_count, block_count, block_len, state_dim)
    c_blocks = c_rows.reshape(seq_count, block_count, block_len, state_dim)
    dt_blocks = steps_dt.reshape(seq_count, block_count, block_len, heads_here)
    log_decay = jnp.cumsum(dt_blocks * rate, axis=2)
    block_end = log_decay[:, :, -1, :]
    position = jnp.arange(block_len)
    causal = (position[:, None] >= position[None, :])[None, None, :, :, None]
    gaps = log_decay[:, :, :, None, :] - log_decay[:, :, None, :, :]
    decay_mat = jnp.where(causal, jnp.exp(jnp.where(causal, gaps, 0.0)), 0.0)
    scores = jnp.einsum('scin,scjn->scij', c_blocks, b_blocks, precision=highest)
    mixing = scores[..., None] * decay_mat
    x_scaled = x_blocks * dt_blocks[..., None]
    y_inner = jnp.einsum('scijh,scjhp->scihp', mixing, x_scaled, precision=highest)
    to_end = jnp.exp(block_end[:, :, None, :] - log_decay)
    block_states = jnp.einsum('scjn,scjhp->schnp', b_blocks, x_scaled * to_end[..., None], precision=highest)

    def advance(carried, pieces):
        piece_state, piece_end = pieces
        return (carried * jnp.exp(piece_end)[:, :, None, None] + piece_state, carried)
    start_state = jnp.zeros((seq_count, heads_here, state_dim, head_dim), jnp.float32)
    _, entering = lax.scan(advance, start_state, (jnp.moveaxis(block_states, 1, 0), jnp.moveaxis(block_end, 1, 0)))
    entering = jnp.moveaxis(entering, 0, 1)
    y_outer = jnp.einsum('scin,schnp->scihp', c_blocks, entering, precision=highest) * jnp.exp(log_decay)[..., None]
    result = y_inner + y_outer + x_blocks * skip_term[:, None]
    return result.reshape(rows_all, heads_here, head_dim)

def mixer(gate_pre, value_pre, state_pre, step_pre, value_conv, value_conv_bias, state_conv, state_conv_bias, step_bias, decay_log, skip_gain):
    x_conv = jax.nn.silu(causal_conv(value_pre, value_conv, value_conv_bias, SEQLEN))
    bc_conv = jax.nn.silu(causal_conv(state_pre, state_conv, state_conv_bias, SEQLEN))
    steps_dt = jax.nn.softplus(step_pre + step_bias)
    rows_all = x_conv.shape[0]
    scanned = block_scan(x_conv.reshape(rows_all, -1, HEADDIM), bc_conv[:, :NSTATE], bc_conv[:, NSTATE:], steps_dt, -jnp.exp(decay_log), skip_gain, SEQLEN, BLOCK_LEN)
    return scanned.reshape(rows_all, -1) * jax.nn.silu(gate_pre)

def contract_rows(left, right):
    return lax.dot_general(left, right, (((0,), (0,)), ((), ())), preferred_element_type=jnp.float32)

def contract_cols(left, right):
    return lax.dot_general(left, right, (((1,), (1,)), ((), ())), preferred_element_type=jnp.float32)

def reference(block_input, cotangent, norm_gain, gate_proj, value_proj, state_proj, step_proj, value_conv, value_conv_bias, state_conv, state_conv_bias, step_bias, decay_log, skip_gain, mixer_gain, out_proj):
    seq_count = block_input.shape[0] // SEQLEN
    inputs_seq = block_input.reshape(seq_count, SEQLEN, D)
    cot_seq = cotangent.reshape(seq_count, SEQLEN, D)
    params = (norm_gain, gate_proj, value_proj, state_proj, step_proj, value_conv, value_conv_bias, state_conv, state_conv_bias, step_bias, decay_log, skip_gain, mixer_gain, out_proj)
    start_sums = tuple((jnp.zeros(item.shape, jnp.float32) for item in params))

    def one_sequence(sums, pair):
        rows_in, rows_cot = pair
        rms_inv = lax.rsqrt(lax.optimization_barrier(jnp.mean(rows_in * rows_in, axis=1, keepdims=True)) + norm_eps)
        normed = (rows_in * rms_inv * norm_gain).astype(jnp.bfloat16)
        gate_pre = jnp.dot(normed, gate_proj, preferred_element_type=jnp.float32)
        value_pre = jnp.dot(normed, value_proj, preferred_element_type=jnp.float32)
        state_pre = jnp.dot(normed, state_proj, preferred_element_type=jnp.float32)
        step_pre = jnp.dot(normed, step_proj, preferred_element_type=jnp.float32)
        gated, pull_back = jax.vjp(mixer, gate_pre, value_pre, state_pre, step_pre, value_conv, value_conv_bias, state_conv, state_conv_bias, step_bias, decay_log, skip_gain)
        gate_inv = lax.rsqrt(lax.optimization_barrier(jnp.sum(gated * gated, axis=1, keepdims=True)) / INNER + norm_eps)
        mixed_rows = (gated * gate_inv * mixer_gain).astype(jnp.bfloat16)
        outputs = rows_in + jnp.dot(mixed_rows, out_proj, preferred_element_type=jnp.float32)
        cot_low = rows_cot.astype(jnp.bfloat16)
        out_grad = contract_rows(mixed_rows, cot_low)
        mixed_grad = contract_cols(cot_low, out_proj)
        gain_term = lax.optimization_barrier(jnp.sum(mixed_grad * gated * gate_inv, axis=0))
        scaled_grad = mixed_grad * mixer_gain
        row_dot = lax.optimization_barrier(jnp.sum(scaled_grad * gated, axis=1, keepdims=True))
        gated_grad = gate_inv * scaled_grad - gated * gate_inv ** 3 * row_dot / INNER
        pulled = pull_back(gated_grad)
        gate_low = pulled[0].astype(jnp.bfloat16)
        value_low = pulled[1].astype(jnp.bfloat16)
        state_low = pulled[2].astype(jnp.bfloat16)
        step_low = pulled[3].astype(jnp.bfloat16)
        proj_grads = (contract_rows(normed, gate_low), contract_rows(normed, value_low), contract_rows(normed, state_low), contract_rows(normed, step_low))
        normed_grad = contract_cols(gate_low, gate_proj) + contract_cols(value_low, value_proj) + contract_cols(step_low, step_proj) + contract_cols(state_low, state_proj)
        norm_term = lax.optimization_barrier(jnp.sum(normed_grad * rows_in * rms_inv, axis=0))
        scaled_in = normed_grad * norm_gain
        input_rows = rms_inv * scaled_in - rows_in * rms_inv ** 3 * lax.optimization_barrier(jnp.mean(scaled_in * rows_in, axis=1, keepdims=True)) + rows_cot
        terms = (norm_term,) + proj_grads + tuple(pulled[4:]) + (gain_term, out_grad)
        new_sums = tuple((old_item + new_item for old_item, new_item in zip(sums, terms)))
        return (new_sums, (outputs, input_rows))
    sums, (outputs, input_rows) = lax.scan(one_sequence, start_sums, (inputs_seq, cot_seq))
    block_output = outputs.reshape(seq_count * SEQLEN, D)
    input_grad = input_rows.reshape(seq_count * SEQLEN, D)
    return (block_output, input_grad, sums[0], sums[1], sums[2], sums[3], sums[4], sums[5], sums[6], sums[7], sums[8], sums[9], sums[10], sums[11], sums[12], sums[13])
```

```python
import functools

import jax
import jax.numpy as jnp
from jax import lax
from jax.experimental import pallas as pl
from jax.experimental.pallas import tpu as pltpu
from jax.sharding import PartitionSpec as P

HEADDIM = 64
SEQLEN = 1024
CHUNK = 128
ROWS = 256
LANES = 128

norm_eps = 1e-05
bf16 = jnp.bfloat16
f32 = jnp.float32


VMEM_LIMIT = 60 * 1024 * 1024


def dot_nn(a, b):
    return lax.dot_general(a, b, (((1,), (0,)), ((), ())), preferred_element_type=f32)


def dot_nt(a, b):
    return lax.dot_general(a, b, (((1,), (1,)), ((), ())), preferred_element_type=f32)


def dot_tn(a, b):
    return lax.dot_general(a, b, (((0,), (0,)), ((), ())), preferred_element_type=f32)


def sigmoid(v):
    return 1.0 / (1.0 + jnp.exp(-v))


def swap(a, axis, mask):
    size = lax.axis_size(axis)
    return lax.ppermute(a, axis, [(i, i ^ mask) for i in range(size)])


def radices(size):
    bits = size.bit_length() - 1
    out = [2] if bits % 2 else []
    return out + [4] * (bits // 2)


def gather_relative(block, axis, order):
    held = {0: block}
    for masks in order:
        for k, item in list(held.items()):
            for m in masks:
                held[k ^ m] = swap(item, axis, m)
    return [held[k] for k in range(len(held))]


def dp_masks(size):
    groups, low = [], 1
    for r in radices(size):
        groups.append([low * i for i in range(1, r)])
        low *= r
    return groups[::-1]


def take(a, index, axis):
    return lax.dynamic_index_in_dim(a, index, axis, keepdims=False)


def scatter_sum(g, axis, group_radices):
    me = lax.axis_index(axis)
    low = 1
    total = g
    for r in group_radices:
        count = total.shape[0]
        split = total.reshape((count // r, r) + total.shape[1:])
        digit = (me // low) % r
        kept = take(split, digit, 1).astype(f32)
        for m in range(1, r):
            kept = kept + swap(take(split, digit ^ m, 1).astype(bf16), axis, m * low).astype(f32)
        total = kept
        low *= r
    return total[0]


def all_sum(a, axis):
    size, m = lax.axis_size(axis), 1
    while m < size:
        a = a + swap(a, axis, m)
        m *= 2
    return a


def any_spec():
    return pl.BlockSpec(memory_space=pl.ANY)


def smem_spec():
    return pl.BlockSpec(memory_space=pltpu.SMEM)


def full_spec(shape):
    zeros = (0,) * len(shape)
    return pl.BlockSpec(shape, lambda i: zeros)


def rows_spec(rows, cols):
    return pl.BlockSpec((rows, cols), lambda i: (i, 0))


def params():
    return pltpu.CompilerParams(vmem_limit_bytes=VMEM_LIMIT)


def place(blocks, dest, me, sems, base=0):
    rows = blocks[0].shape[0]
    copies = []
    for k, ref in enumerate(blocks):
        at = pl.multiple_of((me ^ k) * rows, rows & -rows)
        copies.append(pltpu.make_async_copy(ref, dest.at[pl.ds(at, rows), :], sems.at[base + k]))
    for c in copies:
        c.start()
    for c in copies:
        c.wait()


def causal_taps(buf, rows, conv, bias):
    taps = conv.shape[0]
    total = bias
    for k in range(taps):
        total = total + buf[pl.ds(8 - (taps - 1) + k, rows), :] * conv[k : k + 1, :]
    return total


def tri(rows, upper):
    i = lax.broadcasted_iota(jnp.int32, (rows, rows), 0)
    j = lax.broadcasted_iota(jnp.int32, (rows, rows), 1)
    return jnp.where(i <= j if upper else i >= j, 1.0, 0.0).astype(f32)


def small_kernel(nb, ns, me_ref, *refs):
    normed_blocks, small_blocks = refs[:nb], refs[nb : nb + ns]
    conv, cbias, sbias, rate = refs[nb + ns : nb + ns + 4]
    normed, wst, state_pre, u_out, bc, step_v, cum, halo, sems = refs[nb + ns + 4 :]
    i = pl.program_id(0)
    cols = conv.shape[1]

    @pl.when(i == 0)
    def _():
        place(normed_blocks, normed, me_ref[1], sems)
        place(small_blocks, wst, me_ref[0], sems, nb)

    @pl.when(i % (SEQLEN // ROWS) == 0)
    def _():
        halo[0:8, :] = jnp.zeros((8, cols), f32)

    at = pl.multiple_of(i * ROWS, ROWS)
    pre = dot_nn(normed[pl.ds(at, ROWS), :], wst[...])
    state_pre[...] = pre[:, :cols]
    halo[pl.ds(8, ROWS), :] = pre[:, :cols]
    u = causal_taps(halo, ROWS, conv[...], cbias[...])
    halo[0:8, :] = halo[pl.ds(ROWS, 8), :]
    u_out[...] = u
    bc[...] = (u * sigmoid(u)).astype(bf16)
    v = pre[:, cols:] + sbias[...]
    step_v[...] = v
    a = (jnp.maximum(v, 0.0) + jnp.log1p(jnp.exp(-jnp.abs(v)))) * rate[...]
    low = tri(CHUNK, False)
    for c in range(ROWS // CHUNK):
        part = a[c * CHUNK : (c + 1) * CHUNK, :]
        cum[c * CHUNK : (c + 1) * CHUNK, :] = lax.dot_general(
            low, part, (((1,), (0,)), ((), ())), precision=lax.Precision.HIGHEST, preferred_element_type=f32
        )


def small_call(me, normed_blocks, small_blocks, conv, cbias, sbias, rate):
    nb, ns = len(normed_blocks), len(small_blocks)
    r, depth = normed_blocks[0].shape
    tokens = nb * r
    wide = small_blocks[0].shape[1]
    cols = conv.shape[1]
    out_shape = (
        jax.ShapeDtypeStruct((tokens, depth), bf16),
        jax.ShapeDtypeStruct((depth, wide), bf16),
        jax.ShapeDtypeStruct((tokens, cols), f32),
        jax.ShapeDtypeStruct((tokens, cols), f32),
        jax.ShapeDtypeStruct((tokens, cols), bf16),
        jax.ShapeDtypeStruct((tokens, LANES), f32),
        jax.ShapeDtypeStruct((tokens, LANES), f32),
    )
    return pl.pallas_call(
        functools.partial(small_kernel, nb, ns),
        grid=(tokens // ROWS,),
        in_specs=[smem_spec()]
        + [any_spec()] * (nb + ns)
        + [full_spec(conv.shape), full_spec(cbias.shape), full_spec(sbias.shape), full_spec(rate.shape)],
        out_specs=(
            full_spec((tokens, depth)),
            full_spec((depth, wide)),
            rows_spec(ROWS, cols),
            rows_spec(ROWS, cols),
            rows_spec(ROWS, cols),
            rows_spec(ROWS, LANES),
            rows_spec(ROWS, LANES),
        ),
        out_shape=out_shape,
        scratch_shapes=[pltpu.VMEM((ROWS + 8, cols), f32), pltpu.SemaphoreType.DMA((nb + ns,))],
        compiler_params=params(),
        name="small_proj",
        cost_estimate=pl.CostEstimate(
            flops=2 * tokens * depth * wide, bytes_accessed=12 * 1024 * 1024, transcendentals=0
        ),
    )(me, *normed_blocks, *small_blocks, conv, cbias, sbias, rate)


def lane_half():
    return lax.broadcasted_iota(jnp.int32, (CHUNK, LANES), 1) < HEADDIM


def column(a, h):
    return jnp.broadcast_to(a[:, h : h + 1], (CHUNK, LANES))


def scan_fwd_kernel(ns, me_ref, *refs):
    blocks = refs[:ns]
    normed, conv, cbias, skip, bc, step_v, cum = refs[ns : ns + 7]
    w_out, value_pre, u_out, y_out, entering, halo, state, x_buf, sems = refs[ns + 7 :]
    i = pl.program_id(0)
    cols = conv.shape[1]
    nstate = bc.shape[1] // 2
    pairs = cols // LANES

    @pl.when(i == 0)
    def _():
        place(blocks, w_out, me_ref[0], sems)

    @pl.when(i % (SEQLEN // ROWS) == 0)
    def _():
        halo[0:8, :] = jnp.zeros((8, cols), f32)
        state[...] = jnp.zeros_like(state)

    pre = dot_nn(normed[...], w_out[...])
    value_pre[...] = pre
    halo[pl.ds(8, ROWS), :] = pre
    u = causal_taps(halo, ROWS, conv[...], cbias[...])
    halo[0:8, :] = halo[pl.ds(ROWS, 8), :]
    u_out[...] = u
    x_buf[...] = u * sigmoid(u)

    first = lane_half()
    ci = lax.broadcasted_iota(jnp.int32, (CHUNK, CHUNK), 0)
    cj = lax.broadcasted_iota(jnp.int32, (CHUNK, CHUNK), 1)
    causal = ci >= cj

    def chunk(c, carry):
        at = pl.multiple_of(c * CHUNK, CHUNK)
        b = bc[pl.ds(at, CHUNK), :nstate]
        cc = bc[pl.ds(at, CHUNK), nstate:]
        bt = b.astype(f32).T.astype(bf16)
        scores = dot_nt(cc, b)
        cumc = cum[pl.ds(at, CHUNK), :]
        cumt = cumc.T
        v = step_v[pl.ds(at, CHUNK), :]
        dt = jnp.maximum(v, 0.0) + jnp.log1p(jnp.exp(-jnp.abs(v)))
        for g in range(pairs):
            lanes = slice(g * LANES, (g + 1) * LANES)
            c0, c1 = column(cumc, 2 * g), column(cumc, 2 * g + 1)
            m0 = scores * jnp.exp(jnp.where(causal, c0 - cumt[2 * g : 2 * g + 1, :], -1e30))
            m1 = scores * jnp.exp(jnp.where(causal, c1 - cumt[2 * g + 1 : 2 * g + 2, :], -1e30))
            m2 = jnp.concatenate([m0.astype(bf16), m1.astype(bf16)], axis=1)
            cumx = jnp.where(first, c0, c1)
            dtx = jnp.where(first, column(dt, 2 * g), column(dt, 2 * g + 1))
            x = x_buf[pl.ds(at, CHUNK), lanes]
            xs = x * dtx
            x2 = jnp.concatenate([jnp.where(first, xs, 0.0).astype(bf16), jnp.where(first, 0.0, xs).astype(bf16)], axis=0)
            s = state[:, lanes]
            sb = s.astype(bf16)
            entering[c, :, lanes] = sb
            y = dot_nn(m2, x2) + dot_nn(cc, sb) * jnp.exp(cumx) + x * skip[:, lanes]
            y_out[pl.ds(at, CHUNK), lanes] = y
            endx = cumx[CHUNK - 1 : CHUNK, :]
            state[:, lanes] = s * jnp.exp(endx) + dot_nn(bt, (xs * jnp.exp(endx - cumx)).astype(bf16))
        return carry

    lax.fori_loop(0, ROWS // CHUNK, chunk, 0)


def scan_fwd_call(me, blocks, normed, conv, cbias, skip, bc, step_v, cum):
    ns = len(blocks)
    tokens, depth = normed.shape
    cols = conv.shape[1]
    nstate = bc.shape[1] // 2
    chunks = tokens // CHUNK
    per = ROWS // CHUNK
    return pl.pallas_call(
        functools.partial(scan_fwd_kernel, ns),
        grid=(tokens // ROWS,),
        in_specs=[smem_spec()]
        + [any_spec()] * ns
        + [
            rows_spec(ROWS, depth),
            full_spec(conv.shape),
            full_spec(cbias.shape),
            full_spec(skip.shape),
            rows_spec(ROWS, 2 * nstate),
            rows_spec(ROWS, LANES),
            rows_spec(ROWS, LANES),
        ],
        out_specs=(
            full_spec((depth, cols)),
            rows_spec(ROWS, cols),
            rows_spec(ROWS, cols),
            rows_spec(ROWS, cols),
            pl.BlockSpec((per, nstate, cols), lambda i: (i, 0, 0)),
        ),
        out_shape=(
            jax.ShapeDtypeStruct((depth, cols), bf16),
            jax.ShapeDtypeStruct((tokens, cols), f32),
            jax.ShapeDtypeStruct((tokens, cols), f32),
            jax.ShapeDtypeStruct((tokens, cols), f32),
            jax.ShapeDtypeStruct((chunks, nstate, cols), bf16),
        ),
        scratch_shapes=[
            pltpu.VMEM((ROWS + 8, cols), f32),
            pltpu.VMEM((nstate, cols), f32),
            pltpu.VMEM((ROWS, cols), f32),
            pltpu.SemaphoreType.DMA((ns,)),
        ],
        compiler_params=params(),
        name="scan_fwd",
        cost_estimate=pl.CostEstimate(
            flops=4 * tokens * depth * cols, bytes_accessed=20 * 1024 * 1024, transcendentals=0
        ),
    )(me, *blocks, normed, conv, cbias, skip, bc, step_v, cum)


def row_form(col):
    parts = []
    for c in range(ROWS // CHUNK):
        wide = jnp.broadcast_to(col[c * CHUNK : (c + 1) * CHUNK, :], (CHUNK, LANES))
        parts.append(wide.T[0:8, :][None])
    return jnp.concatenate(parts, axis=0)


def col_form(rows, cols):
    parts = [jnp.broadcast_to(rows[c, 0:1, :], (CHUNK, LANES)).T for c in range(rows.shape[0])]
    tall = jnp.concatenate(parts, axis=0)
    return jnp.concatenate([tall] * (cols // LANES), axis=1)


def gate_kernel(ns, me_ref, *refs):
    blocks = refs[:ns]
    normed, y, w_out, gate_pre, gated_out, squares, sems = refs[ns:]

    @pl.when(pl.program_id(0) == 0)
    def _():
        place(blocks, w_out, me_ref[0], sems)

    pre = dot_nn(normed[...], w_out[...])
    gate_pre[...] = pre
    gated = y[...] * (pre * sigmoid(pre))
    gated_out[...] = gated
    squares[...] = row_form(jnp.sum(gated * gated, axis=1, keepdims=True))


def stat_spec():
    return pl.BlockSpec((ROWS // CHUNK, 8, LANES), lambda i: (i, 0, 0))


def gate_call(me, blocks, normed, y):
    ns = len(blocks)
    tokens, depth = normed.shape
    cols = y.shape[1]
    return pl.pallas_call(
        functools.partial(gate_kernel, ns),
        grid=(tokens // ROWS,),
        in_specs=[smem_spec()] + [any_spec()] * ns + [rows_spec(ROWS, depth), rows_spec(ROWS, cols)],
        out_specs=(full_spec((depth, cols)), rows_spec(ROWS, cols), rows_spec(ROWS, cols), stat_spec()),
        out_shape=(
            jax.ShapeDtypeStruct((depth, cols), bf16),
            jax.ShapeDtypeStruct((tokens, cols), f32),
            jax.ShapeDtypeStruct((tokens, cols), f32),
            jax.ShapeDtypeStruct((tokens // CHUNK, 8, LANES), f32),
        ),
        scratch_shapes=[pltpu.SemaphoreType.DMA((ns,))],
        compiler_params=params(),
        name="gate_proj",
        cost_estimate=pl.CostEstimate(
            flops=2 * tokens * depth * cols, bytes_accessed=16 * 1024 * 1024, transcendentals=0
        ),
    )(me, *blocks, normed, y)


def mixed_kernel(inner, nb, me_ref, *refs):
    blocks = refs[:nb]
    gated, squares, gain, mixed, cot, sems = refs[nb:]

    @pl.when(pl.program_id(0) == 0)
    def _():
        place(blocks, cot, me_ref[1], sems)

    inv = lax.rsqrt(col_form(squares[...], gated.shape[1]) / inner + norm_eps)
    mixed[...] = (gated[...] * inv * gain[...]).astype(bf16)


def mixed_call(me, cot_blocks, gated, squares, gain, inner):
    tokens, cols = gated.shape
    nb = len(cot_blocks)
    depth = cot_blocks[0].shape[1]
    return pl.pallas_call(
        functools.partial(mixed_kernel, inner, nb),
        grid=(tokens // ROWS,),
        in_specs=[smem_spec()] + [any_spec()] * nb + [rows_spec(ROWS, cols), stat_spec(), full_spec(gain.shape)],
        out_specs=(rows_spec(ROWS, cols), full_spec((tokens, depth))),
        out_shape=(jax.ShapeDtypeStruct((tokens, cols), bf16), jax.ShapeDtypeStruct((tokens, depth), bf16)),
        scratch_shapes=[pltpu.SemaphoreType.DMA((nb,))],
        compiler_params=params(),
        name="mixed_rows",
        cost_estimate=pl.CostEstimate(flops=0, bytes_accessed=8 * 1024 * 1024, transcendentals=0),
    )(me, *cot_blocks, gated, squares, gain)


def out_kernel(ns, me_ref, *refs):
    blocks = refs[:ns]
    cot, gated, gain, w_out, mixed_grad, dots, sems = refs[ns:]

    @pl.when(pl.program_id(0) == 0)
    def _():
        place(blocks, w_out, me_ref[0], sems)

    grad = dot_nn(cot[...], w_out[...])
    mixed_grad[...] = grad
    dots[...] = row_form(jnp.sum(grad * gain[...] * gated[...], axis=1, keepdims=True))


def out_call(me, blocks, cot, gated, gain):
    ns = len(blocks)
    tokens, depth = cot.shape
    cols = gated.shape[1]
    return pl.pallas_call(
        functools.partial(out_kernel, ns),
        grid=(tokens // ROWS,),
        in_specs=[smem_spec()]
        + [any_spec()] * ns
        + [rows_spec(ROWS, depth), rows_spec(ROWS, cols), full_spec(gain.shape)],
        out_specs=(full_spec((depth, cols)), rows_spec(ROWS, cols), stat_spec()),
        out_shape=(
            jax.ShapeDtypeStruct((depth, cols), bf16),
            jax.ShapeDtypeStruct((tokens, cols), f32),
            jax.ShapeDtypeStruct((tokens // CHUNK, 8, LANES), f32),
        ),
        scratch_shapes=[pltpu.SemaphoreType.DMA((ns,))],
        compiler_params=params(),
        name="mixed_grad",
        cost_estimate=pl.CostEstimate(
            flops=2 * tokens * depth * cols, bytes_accessed=16 * 1024 * 1024, transcendentals=0
        ),
    )(me, *blocks, cot, gated, gain)


def fold(a):
    return a.reshape(a.shape[0] // 8, 8, a.shape[1]).sum(axis=0)


def gated_grad_kernel(inner, mixed_grad, gate_pre, y, squares, dots, gain, gate_low, y_grad, gain_grad):
    cols = y.shape[1]

    @pl.when(pl.program_id(0) == 0)
    def _():
        gain_grad[...] = jnp.zeros_like(gain_grad)

    inv = lax.rsqrt(col_form(squares[...], cols) / inner + norm_eps)
    dot = col_form(dots[...], cols)
    pre, ys, grad = gate_pre[...], y[...], mixed_grad[...]
    sig = sigmoid(pre)
    silu = pre * sig
    gated = ys * silu
    gain_grad[...] += fold(grad * gated * inv)
    gg = inv * (grad * gain[...]) - gated * (inv * inv * inv) * dot / inner
    y_grad[...] = gg * silu
    gate_low[...] = (gg * ys * (sig * (1.0 + pre * (1.0 - sig)))).astype(bf16)


def gated_grad_call(mixed_grad, gate_pre, y, squares, dots, gain, inner):
    tokens, cols = y.shape
    big = rows_spec(ROWS, cols)
    return pl.pallas_call(
        functools.partial(gated_grad_kernel, inner),
        grid=(tokens // ROWS,),
        in_specs=[big, big, big, stat_spec(), stat_spec(), full_spec(gain.shape)],
        out_specs=(big, big, full_spec((8, cols))),
        out_shape=(
            jax.ShapeDtypeStruct((tokens, cols), bf16),
            jax.ShapeDtypeStruct((tokens, cols), f32),
            jax.ShapeDtypeStruct((8, cols), f32),
        ),
        compiler_params=params(),
        name="gated_grad",
        cost_estimate=pl.CostEstimate(flops=0, bytes_accessed=14 * 1024 * 1024, transcendentals=0),
    )(mixed_grad, gate_pre, y, squares, dots, gain)


def scan_bwd_kernel(
    y_grad, u_in, value_pre, entering, bc, us, state_pre, step_v, cum, conv, sconv, skip, rate,
    value_low, small_low, sums_v, sums_s, sums_h,
    du_buf, ds_buf, carried, x_buf, dx_buf, sem_acc,
):
    i = pl.program_id(0)
    cols = conv.shape[1]
    scols = sconv.shape[1]
    nstate = scols // 2
    pairs = cols // LANES
    taps = conv.shape[0]

    @pl.when(i == 0)
    def _():
        sums_v[...] = jnp.zeros_like(sums_v)
        sums_s[...] = jnp.zeros_like(sums_s)
        sums_h[...] = jnp.zeros_like(sums_h)

    @pl.when(i % (SEQLEN // CHUNK) == 0)
    def _():
        du_buf[pl.ds(CHUNK, 8), :] = jnp.zeros((8, cols), f32)
        ds_buf[pl.ds(CHUNK, 8), :] = jnp.zeros((8, scols), f32)
        carried[...] = jnp.zeros_like(carried)

    first = lane_half()
    ci = lax.broadcasted_iota(jnp.int32, (CHUNK, CHUNK), 0)
    cj = lax.broadcasted_iota(jnp.int32, (CHUNK, CHUNK), 1)
    causal = ci >= cj
    strict = ci > cj

    u = u_in[...]
    sig = sigmoid(u)
    x_buf[...] = u * sig

    b = bc[:, :nstate]
    cc = bc[:, nstate:]
    ct = cc.astype(f32).T.astype(bf16)
    scores = dot_nt(cc, b)
    cumc = cum[...]
    cumt = cumc.T
    v = step_v[...]
    dt = jnp.maximum(v, 0.0) + jnp.log1p(jnp.exp(-jnp.abs(v)))

    dscores = jnp.zeros((CHUNK, CHUNK), f32)
    db = jnp.zeros((CHUNK, nstate), f32)
    dc = jnp.zeros((CHUNK, nstate), f32)
    rowacc = jnp.zeros((CHUNK, LANES), f32)
    sem_acc[...] = jnp.zeros_like(sem_acc)
    colsums = []
    ends = jnp.zeros((8, LANES), f32)
    for g in range(pairs):
        lanes = slice(g * LANES, (g + 1) * LANES)
        c0, c1 = column(cumc, 2 * g), column(cumc, 2 * g + 1)
        d0 = jnp.exp(jnp.where(causal, c0 - cumt[2 * g : 2 * g + 1, :], -1e30))
        d1 = jnp.exp(jnp.where(causal, c1 - cumt[2 * g + 1 : 2 * g + 2, :], -1e30))
        m2 = jnp.concatenate([(scores * d0), (scores * d1)], axis=1)
        m2t = m2.T.astype(bf16)
        cumx = jnp.where(first, c0, c1)
        ex = jnp.exp(cumx)
        endx = cumx[CHUNK - 1 : CHUNK, :]
        toend = jnp.exp(endx - cumx)
        dtx = jnp.where(first, column(dt, 2 * g), column(dt, 2 * g + 1))
        x = x_buf[:, lanes]
        xs = x * dtx
        x2 = jnp.concatenate([jnp.where(first, xs, 0.0).astype(bf16), jnp.where(first, 0.0, xs).astype(bf16)], axis=0)
        dy = y_grad[:, lanes]
        dyb = dy.astype(bf16)
        dm = dot_nt(dyb, x2)
        t0 = dm[:, :CHUNK] * d0
        t1 = dm[:, CHUNK:] * d1
        dscores = dscores + t0 + t1
        g0 = jnp.where(strict, t0 * scores, 0.0)
        g1 = jnp.where(strict, t1 * scores, 0.0)
        rowacc = jnp.where(cj == 2 * g, jnp.sum(g0, axis=1, keepdims=True), rowacc)
        rowacc = jnp.where(cj == 2 * g + 1, jnp.sum(g1, axis=1, keepdims=True), rowacc)
        colsums += [jnp.sum(g0, axis=0, keepdims=True), jnp.sum(g1, axis=0, keepdims=True)]
        both = dot_nn(m2t, dyb)
        ds = carried[:, lanes]
        dsb = ds.astype(bf16)
        sin = entering[0, :, lanes]
        bds = dot_nn(b, dsb) * toend
        dxs = jnp.where(first, both[:CHUNK, :], both[CHUNK:, :]) + bds
        dye = dy * ex
        dyeb = dye.astype(bf16)
        yo = dot_nn(cc, sin)
        xe = (xs * toend).astype(bf16)
        db = db + dot_nt(xe, dsb)
        dc = dc + dot_nt(dyeb, sin)
        ends_here = jnp.exp(endx) * jnp.sum(fold(sin.astype(f32) * ds), axis=0, keepdims=True)
        spread = jnp.where((cj == 2 * g + jnp.where(ci >= HEADDIM, 1, 0)), 1.0, 0.0).astype(bf16)
        stacked = jnp.concatenate([(dye * yo).astype(bf16), (xs * bds).astype(bf16), (dxs * x).astype(bf16)], axis=0)
        sem_acc[...] += dot_nn(stacked, spread)
        ends = ends + dot_nn(jnp.broadcast_to(ends_here, (8, LANES)), spread.astype(f32))
        carried[:, lanes] = ds * jnp.exp(endx) + dot_nn(ct, dyeb)
        dx_buf[:, lanes] = dxs * dtx + dy * skip[:, lanes]
        sums_v[5, :, lanes] += fold(dy * x)

    dsb16 = dscores.astype(bf16)
    db = db + dot_nn(dscores.T.astype(bf16), cc)
    dc = dc + dot_nn(dsb16, b)

    pad = jnp.zeros((LANES - len(colsums), CHUNK), f32)
    colt = jnp.concatenate(colsums + [pad], axis=0).T
    qsum = sem_acc[pl.ds(CHUNK, CHUNK), :]
    dcum = rowacc - colt + sem_acc[pl.ds(0, CHUNK), :] - qsum
    dend = ends[0:1, :] + jnp.sum(fold(qsum), axis=0, keepdims=True)
    dcum = dcum + jnp.where(ci == CHUNK - 1, dend, 0.0)
    da = lax.dot_general(
        tri(CHUNK, True), dcum, (((1,), (0,)), ((), ())), precision=lax.Precision.HIGHEST, preferred_element_type=f32
    )
    ddt = sem_acc[pl.ds(2 * CHUNK, CHUNK), :] + da * rate[...]
    dv = ddt * sigmoid(v)
    small_low[:, scols:] = dv.astype(bf16)
    sums_h[0, :, :] += fold(dv)
    sums_h[1, :, :] += fold(da * dt) * rate[...]

    du = dx_buf[...] * (sig * (1.0 + u * (1.0 - sig)))
    du_buf[pl.ds(0, CHUNK), :] = du
    pre = value_pre[...]
    total = jnp.zeros((CHUNK, cols), f32)
    for k in range(taps):
        part = du_buf[pl.ds(taps - 1 - k, CHUNK), :]
        total = total + part * conv[k : k + 1, :]
        sums_v[k, :, :] += fold(part * pre)
    sums_v[4, :, :] += fold(du)
    value_low[...] = total.astype(bf16)
    du_buf[pl.ds(CHUNK, 8), :] = du[0:8, :]

    uu = us[...]
    sg = sigmoid(uu)
    du = jnp.concatenate([db, dc], axis=1) * (sg * (1.0 + uu * (1.0 - sg)))
    ds_buf[pl.ds(0, CHUNK), :] = du
    pre = state_pre[...]
    total = jnp.zeros((CHUNK, scols), f32)
    for k in range(taps):
        part = ds_buf[pl.ds(taps - 1 - k, CHUNK), :]
        total = total + part * sconv[k : k + 1, :]
        sums_s[k, :, :] += fold(part * pre)
    sums_s[4, :, :] += fold(du)
    small_low[:, :scols] = total.astype(bf16)
    ds_buf[pl.ds(CHUNK, 8), :] = du[0:8, :]


def scan_bwd_call(y_grad, u, value_pre, entering, bc, us, state_pre, step_v, cum, conv, sconv, skip, rate):
    tokens, cols = y_grad.shape
    scols = us.shape[1]
    nstate = scols // 2
    chunks = tokens // CHUNK

    def back(width):
        return pl.BlockSpec((CHUNK, width), lambda i: (chunks - 1 - i, 0))

    return pl.pallas_call(
        scan_bwd_kernel,
        grid=(chunks,),
        in_specs=[
            back(cols),
            back(cols),
            back(cols),
            pl.BlockSpec((1, nstate, cols), lambda i: (chunks - 1 - i, 0, 0)),
            back(scols),
            back(scols),
            back(scols),
            back(LANES),
            back(LANES),
            full_spec(conv.shape),
            full_spec(sconv.shape),
            full_spec(skip.shape),
            full_spec(rate.shape),
        ],
        out_specs=(
            back(cols),
            back(scols + LANES),
            full_spec((6, 8, cols)),
            full_spec((5, 8, scols)),
            full_spec((2, 8, LANES)),
        ),
        out_shape=(
            jax.ShapeDtypeStruct((tokens, cols), bf16),
            jax.ShapeDtypeStruct((tokens, scols + LANES), bf16),
            jax.ShapeDtypeStruct((6, 8, cols), f32),
            jax.ShapeDtypeStruct((5, 8, scols), f32),
            jax.ShapeDtypeStruct((2, 8, LANES), f32),
        ),
        scratch_shapes=[
            pltpu.VMEM((CHUNK + 8, cols), f32),
            pltpu.VMEM((CHUNK + 8, scols), f32),
            pltpu.VMEM((nstate, cols), f32),
            pltpu.VMEM((CHUNK, cols), f32),
            pltpu.VMEM((CHUNK, cols), f32),
            pltpu.VMEM((3 * CHUNK, LANES), f32),
        ],
        compiler_params=params(),
        name="scan_bwd",
        cost_estimate=pl.CostEstimate(
            flops=8 * tokens * 1024 * cols, bytes_accessed=24 * 1024 * 1024, transcendentals=0
        ),
    )(y_grad, u, value_pre, entering, bc, us, state_pre, step_v, cum, conv, sconv, skip, rate)


def pad_lanes(a):
    return jnp.pad(a, ((0, 0), (0, LANES - a.shape[1])))


def shards(
    block_input,
    cotangent,
    norm_gain,
    gate_proj,
    value_proj,
    state_proj,
    step_proj,
    value_conv,
    value_conv_bias,
    state_conv,
    state_conv_bias,
    step_bias,
    decay_log,
    skip_gain,
    mixer_gain,
    out_proj,
):
    dp, tp = lax.axis_size("dp"), lax.axis_size("tensor")
    me = jnp.stack([lax.axis_index("dp"), lax.axis_index("tensor")]).astype(jnp.int32)
    cols = value_proj.shape[1]
    depth = block_input.shape[1]
    heads = step_proj.shape[1]
    scols = state_proj.shape[1]
    inner = cols * tp
    t_order = [[1 << b] for b in range(tp.bit_length() - 1)][::-1]
    d_order = dp_masks(dp)
    d_radix, t_radix = radices(dp), [2] * (tp.bit_length() - 1)

    rms_inv = lax.rsqrt(jnp.mean(block_input * block_input, axis=1, keepdims=True) + norm_eps)
    normed = (block_input * rms_inv * norm_gain).astype(bf16)
    cot_low = cotangent.astype(bf16)
    small_block = jnp.concatenate([state_proj, pad_lanes(step_proj)], axis=1)
    small_blocks = gather_relative(small_block, "dp", d_order)
    normed_blocks = gather_relative(normed, "tensor", t_order)
    value_blocks = gather_relative(value_proj, "dp", d_order)
    gate_blocks = gather_relative(gate_proj, "dp", d_order)
    cot_blocks = gather_relative(cot_low, "tensor", t_order)
    out_blocks = gather_relative(out_proj.T, "dp", d_order)

    rate_row = pad_lanes(-jnp.exp(decay_log)[None])
    skip_row = jnp.repeat(skip_gain, HEADDIM)[None]
    gain_row = mixer_gain[None]
    normed_all, w_small, state_pre, us, bc, step_v, cum = small_call(
        me, normed_blocks, small_blocks, state_conv, state_conv_bias[None], pad_lanes(step_bias[None]), rate_row
    )
    w_value, value_pre, u, y, entering = scan_fwd_call(
        me, value_blocks, normed_all, value_conv, value_conv_bias[None], skip_row, bc, step_v, cum
    )
    w_gate, gate_pre, gated, squares = gate_call(me, gate_blocks, normed_all, y)
    squares = all_sum(squares, "tensor")
    mixed_rows, cot_all = mixed_call(me, cot_blocks, gated, squares, gain_row, inner)
    out_partial = dot_tn(cot_all, mixed_rows).astype(bf16)
    w_out, mixed_grad, dots = out_call(me, out_blocks, cot_all, gated, gain_row)
    dots = all_sum(dots, "tensor")
    gate_low, y_grad, gain_grad = gated_grad_call(mixed_grad, gate_pre, y, squares, dots, gain_row, inner)
    gate_partial = dot_tn(normed_all, gate_low).astype(bf16)
    block_partial = dot_nt(mixed_rows, w_out).astype(bf16)
    rows = block_input.shape[0]
    block_output = block_input + scatter_sum(block_partial.reshape(tp, rows, depth), "tensor", t_radix)
    value_low, small_low, sums_v, sums_s, sums_h = scan_bwd_call(
        y_grad, u, value_pre, entering, bc, us, state_pre, step_v, cum, value_conv, state_conv, skip_row, rate_row
    )
    small_partial = dot_tn(normed_all, small_low).astype(bf16)
    value_partial = dot_tn(normed_all, value_low).astype(bf16)
    normed_partial = (dot_nt(gate_low, w_gate) + dot_nt(value_low, w_value) + dot_nt(small_low, w_small)).astype(bf16)
    normed_grad = scatter_sum(normed_partial.reshape(tp, rows, depth), "tensor", t_radix)

    def to_owner(partial):
        return scatter_sum(partial.reshape(dp, depth // dp, partial.shape[1]), "dp", d_radix)

    out_grad = to_owner(out_partial).T
    gate_grad = to_owner(gate_partial)
    small_grad = to_owner(small_partial)
    value_grad = to_owner(value_partial)
    state_grad = all_sum(small_grad[:, :scols], "tensor")
    step_grad = small_grad[:, scols : scols + heads]

    norm_term = jnp.sum(normed_grad * block_input * rms_inv, axis=0)
    scaled_in = normed_grad * norm_gain
    input_grad = (
        rms_inv * scaled_in
        - block_input * rms_inv**3 * jnp.mean(scaled_in * block_input, axis=1, keepdims=True)
        + cotangent
    )
    sums_v = jnp.sum(sums_v, axis=1)
    heads_rows = jnp.sum(sums_h, axis=1)[:, :heads]
    skip_grad = sums_v[5].reshape(heads, HEADDIM).sum(axis=1)
    local = jnp.concatenate(
        [sums_v[:5].reshape(-1), jnp.sum(gain_grad, axis=0), heads_rows.reshape(-1), skip_grad]
    )
    local = all_sum(local, "dp")
    shared = jnp.concatenate([norm_term, jnp.sum(sums_s, axis=1).reshape(-1)])
    shared = all_sum(all_sum(shared, "tensor"), "dp")
    n = 4 * cols
    return (
        block_output,
        input_grad,
        shared[:depth],
        gate_grad,
        value_grad,
        state_grad,
        step_grad,
        local[:n].reshape(4, cols),
        local[n : n + cols],
        shared[depth : depth + 4 * scols].reshape(4, scols),
        shared[depth + 4 * scols :],
        local[n + 2 * cols : n + 2 * cols + heads],
        local[n + 2 * cols + heads : n + 2 * cols + 2 * heads],
        local[n + 2 * cols + 2 * heads :],
        local[n + cols : n + 2 * cols],
        out_grad,
    )


def solution(mesh):
    in_specs = (
        P(("dp", "tensor"), None),
        P(("dp", "tensor"), None),
        P(),
        P("dp", "tensor"),
        P("dp", "tensor"),
        P("dp", None),
        P("dp", "tensor"),
        P(None, "tensor"),
        P("tensor"),
        P(),
        P(),
        P("tensor"),
        P("tensor"),
        P("tensor"),
        P("tensor"),
        P("tensor", "dp"),
    )
    out_specs = (
        P(("dp", "tensor"), None),
        P(("dp", "tensor"), None),
        P(),
        P("dp", "tensor"),
        P("dp", "tensor"),
        P("dp", None),
        P("dp", "tensor"),
        P(None, "tensor"),
        P("tensor"),
        P(),
        P(),
        P("tensor"),
        P("tensor"),
        P("tensor"),
        P("tensor"),
        P("tensor", "dp"),
    )
    return jax.shard_map(shards, mesh=mesh, in_specs=in_specs, out_specs=out_specs, check_vma=False)
```

```python
import functools

import jax
import jax.numpy as jnp
from jax import lax
from jax.experimental import pallas as pl
from jax.experimental.pallas import tpu as pltpu
from jax.sharding import PartitionSpec as P


HEADDIM = 64
SEQLEN = 1024
CHUNK = 128
ROWS = 256
LANES = 128

norm_eps = 1e-05
bf16 = jnp.bfloat16
f32 = jnp.float32


VMEM_LIMIT = 16 * 1024 * 1024
LOG2E = 1.4426950408889634


def dot_nn(a, b):
    return lax.dot_general(a, b, (((1,), (0,)), ((), ())), preferred_element_type=f32)


def dot_nt(a, b):
    return lax.dot_general(a, b, (((1,), (1,)), ((), ())), preferred_element_type=f32)


def dot_tn(a, b):
    return lax.dot_general(a, b, (((0,), (0,)), ((), ())), preferred_element_type=f32)


def sigmoid(v):
    return 0.5 + 0.5 * jnp.tanh(0.5 * v)


def swap(a, axis, mask):
    size = lax.axis_size(axis)
    return lax.ppermute(a, axis, [(i, i ^ mask) for i in range(size)])


def radices(size):
    bits = size.bit_length() - 1
    out = [2] if bits % 2 else []
    return out + [4] * (bits // 2)


def gather_relative(block, axis, order):
    held = {0: block}
    for masks in order:
        for k, item in list(held.items()):
            for m in masks:
                held[k ^ m] = swap(item, axis, m)
    return [held[k] for k in range(len(held))]


def gather_dp(block, order):
    arrays = gather_relative(block, "dp", order)
    return arrays, plain(len(arrays))


def plain(count):
    return [((k, 0), k, (k, 0), k) for k in range(count)]


def dp_masks(size):
    groups, low = [], 1
    for r in radices(size):
        groups.append([low * i for i in range(1, r)])
        low *= r
    return groups[::-1]


def exchange(a, axis):
    return [a] + [swap(a, axis, k) for k in range(1, lax.axis_size(axis))]


def pair_sum(parts):
    while len(parts) > 1:
        parts = [parts[i] + parts[i + 1] for i in range(0, len(parts), 2)]
    return parts[0]


def any_spec():
    return pl.BlockSpec(memory_space=pltpu.HBM)


def smem_spec():
    return pl.BlockSpec(memory_space=pltpu.SMEM)


def full_spec(shape):
    zeros = (0,) * len(shape)
    return pl.BlockSpec(shape, lambda i: zeros)


def rows_spec(rows, cols):
    return pl.BlockSpec((rows, cols), lambda i: (i, 0))


def params():
    return pltpu.CompilerParams(vmem_limit_bytes=VMEM_LIMIT)


def place(jobs, me):
    z = lax.div(me, 2)
    middle = jnp.logical_or(z == 1, z == 2)
    always, chosen = [], ([], [])
    for blocks, table, dest, sems in jobs:
        rows = dest.shape[0] // len(table)

        def copy(spot, k, n, blocks=blocks, dest=dest, sems=sems, rows=rows):
            at = pl.multiple_of((me ^ k) * rows, rows & -rows)
            piece = blocks[spot[0]].at[pl.ds(spot[1] * rows, rows), :]
            return pltpu.make_async_copy(piece, dest.at[pl.ds(at, rows), :], sems.at[n])

        for n, (i, k, j, m) in enumerate(table):
            if i == j:
                always.append(functools.partial(copy, i, k, n))
            else:
                chosen[0].append(functools.partial(copy, i, k, n))
                chosen[1].append(functools.partial(copy, j, m, n))
    started = [make() for make in always]
    for c in started:
        c.start()
    for makes, when in zip(chosen, (middle, jnp.logical_not(middle))):
        if makes:

            @pl.when(when)
            def _(makes=makes):
                copies = [make() for make in makes]
                for c in copies:
                    c.start()
                for c in copies:
                    c.wait()

    for c in started:
        c.wait()


def vmem_spec():
    return pl.BlockSpec(memory_space=pltpu.VMEM)


def cost(flops, mib):
    return pl.CostEstimate(flops=flops, bytes_accessed=mib * 1024 * 1024, transcendentals=0)


def norm_kernel(x_hbm, cot_hbm, gain, normed, cot_low, x_buf, cot_buf, sems):
    pieces = x_buf.shape[0] // CHUNK
    spans = [pl.ds(p * CHUNK, CHUNK) for p in range(pieces)]
    loads = [pltpu.make_async_copy(x_hbm.at[s, :], x_buf.at[s, :], sems.at[0, p]) for p, s in enumerate(spans)]
    loads += [pltpu.make_async_copy(cot_hbm.at[s, :], cot_buf.at[s, :], sems.at[1, p]) for p, s in enumerate(spans)]
    for c in loads:
        c.start()
    for p, s in enumerate(spans):
        loads[p].wait()
        x = x_buf[s, :]
        inv = lax.rsqrt(jnp.mean(x * x, axis=1, keepdims=True) + norm_eps)
        normed[s, :] = (x * inv * gain[...]).astype(bf16)
    for p, s in enumerate(spans):
        loads[pieces + p].wait()
        cot_low[s, :] = cot_buf[s, :].astype(bf16)


def norm_call(x, cot, gain):
    rows, depth = x.shape
    out = jax.ShapeDtypeStruct((rows, depth), bf16)
    return pl.pallas_call(
        norm_kernel,
        in_specs=[any_spec(), any_spec(), vmem_spec()],
        out_specs=(vmem_spec(), vmem_spec()),
        out_shape=(out, out),
        scratch_shapes=[
            pltpu.VMEM((rows, depth), f32),
            pltpu.VMEM((rows, depth), f32),
            pltpu.SemaphoreType.DMA((2, rows // CHUNK)),
        ],
        compiler_params=params(),
        name="pre_norm",
        cost_estimate=cost(0, 5),
    )(x, cot, gain)


def tn_kernel(rows, me_ref, a, *refs):
    bs, sent, kept = refs[:-2], refs[-2], refs[-1]
    first = lax.rem(me_ref[0], 2) == 0
    at = 0
    for b in bs:
        lanes = slice(at, at + b.shape[1])
        both = dot_tn(a[...], b[...]).astype(bf16)
        for p in range(sent.shape[0]):
            low, high = both[2 * p * rows : (2 * p + 1) * rows, :], both[(2 * p + 1) * rows : (2 * p + 2) * rows, :]

            @pl.when(first)
            def _(p=p, lanes=lanes, low=low, high=high):
                kept[p, :, lanes] = low
                sent[p, :, lanes] = high

            @pl.when(jnp.logical_not(first))
            def _(p=p, lanes=lanes, low=low, high=high):
                kept[p, :, lanes] = high
                sent[p, :, lanes] = low

        at += b.shape[1]


def tn_call(me, a, bs, dp):
    tokens, depth = a.shape
    cols = sum(b.shape[1] for b in bs)
    rows = depth // dp
    wide = 3 * LANES
    per = wide // (2 * rows)
    out = jax.ShapeDtypeStruct((dp // 2, rows, cols), bf16)
    spec = pl.BlockSpec((per, rows, cols), lambda i: (i, 0, 0))
    return pl.pallas_call(
        functools.partial(tn_kernel, rows),
        grid=(depth // wide,),
        in_specs=[smem_spec(), pl.BlockSpec((tokens, wide), lambda i: (0, i))] + [full_spec(b.shape) for b in bs],
        out_specs=(spec, spec),
        out_shape=(out, out),
        compiler_params=params(),
        name="weight_grad",
        cost_estimate=cost(2 * tokens * depth * cols, 7),
    )(me, a, *bs)


def mid_kernel(axis, low, r, nr, me_ref, *refs):
    kept, received = refs[0], refs[1 : 1 + nr]
    keep, sends = refs[1 + nr], refs[2 + nr :]
    digit = lax.rem(lax.div(me_ref[axis], low), r)
    for o in range(kept.shape[0] // r):
        for m in range(r):
            at = o * r + (digit ^ m)
            total = kept[at].astype(f32)
            for got in received:
                total = total + got[at].astype(f32)
            if m:
                sends[m - 1][o] = total.astype(bf16)
            else:
                keep[o] = total


def mid_call(me, axis, low, r, kept, received):
    count, rows, cols = kept.shape
    shape = (count // r, rows, cols)
    out = pl.pallas_call(
        functools.partial(mid_kernel, axis, low, r, len(received)),
        in_specs=[smem_spec()] + [vmem_spec()] * (1 + len(received)),
        out_specs=(vmem_spec(),) * r,
        out_shape=(jax.ShapeDtypeStruct(shape, f32),) + (jax.ShapeDtypeStruct(shape, bf16),) * (r - 1),
        compiler_params=params(),
        name="partial_sums",
        cost_estimate=cost(0, 4),
    )(me, kept, *received)
    return out[0], list(out[1:])


def finish(me, axis_name, axis, group_radices, sent, kept):
    received = [swap(sent, axis_name, 1)]
    low = 2
    for r in group_radices[1:]:
        kept, sends = mid_call(me, axis, low, r, kept, received)
        received = [swap(item, axis_name, m * low) for m, item in enumerate(sends, 1)]
        low *= r
    return [kept[0]] + [item[0] for item in received]


def total_kernel(count, base, *refs):
    out = refs[-1]
    cols = refs[base].shape[1]
    for n in range((len(refs) - 1 - base) // count):
        terms = refs[base + n * count : base + (n + 1) * count]
        total = refs[0][...] if base else terms[0][...].astype(f32)
        for item in terms[0 if base else 1 :]:
            total = total + item[...].astype(f32)
        out[:, n * cols : (n + 1) * cols] = total


def total_of(groups, base=None):
    rows, cols = groups[0][0].shape
    terms = [item for group in groups for item in group]
    first = [] if base is None else [base]
    return pl.pallas_call(
        functools.partial(total_kernel, len(groups[0]), len(first)),
        in_specs=[vmem_spec()] * (len(first) + len(terms)),
        out_specs=vmem_spec(),
        out_shape=jax.ShapeDtypeStruct((rows, len(groups) * cols), f32),
        compiler_params=params(),
        name="total",
        cost_estimate=cost(0, 4),
    )(*first, *terms)


def rows_kernel(count, norm, me_ref, *refs):
    lows, ws = refs[:count], refs[count : 2 * count]
    total = dot_nt(lows[0][...], ws[0][...])
    for low, w in zip(lows[1:], ws[1:]):
        total = total + dot_nt(low[...], w[...])
    if norm is None:
        refs[2 * count][0] = total.astype(bf16)
        return
    i, last = pl.program_id(0), pl.num_programs(0) - 1
    if norm == "first":
        normed, out, sums = refs[2 * count :]
        out[0] = total.astype(bf16)

        @pl.when(i == 0)
        def _():
            sums[...] = jnp.zeros_like(sums)

        sums[...] += fold(total * normed[...].astype(f32))
        return
    normed, before, state_rows, gain, out, shared, sums = refs[2 * count :]
    out[0] = total.astype(bf16)

    @pl.when(i == 0)
    def _():
        sums[...] = before[...]

    sums[...] += fold(total * normed[...].astype(f32))

    @pl.when(i == last)
    def _():
        half = gain.shape[1] // 2
        row = jnp.sum(sums[...], axis=0, keepdims=True) / gain[...]
        shared[...] = state_rows[...]
        shared[0:1, :] = row[:, :half]
        shared[1:2, :] = row[:, half:]


def rows_call(me, own, lows, ws, tp, norm=None, extra=()):
    tokens = lows[0].shape[0]
    depth = ws[0].shape[0]
    rows = tokens // tp
    half = depth // 2

    def at(i, me_ref):
        bit = lax.rem(me_ref[1], 2)
        return (2 * i + (bit if own else 1 - bit), 0)

    def whole(shape):
        zeros = (0,) * len(shape)
        return pl.BlockSpec(shape, lambda i, me_ref: zeros)

    in_specs = [pl.BlockSpec((rows, low.shape[1]), at) for low in lows] + [whole(w.shape) for w in ws]
    out_specs = [pl.BlockSpec((1, rows, depth), lambda i, me_ref: (i, 0, 0))]
    out_shape = [jax.ShapeDtypeStruct((tp // 2, rows, depth), bf16)]
    scratch = []
    if norm:
        in_specs.append(pl.BlockSpec((rows, depth), at))
    if norm == "first":
        out_specs.append(whole((8, depth)))
        out_shape.append(jax.ShapeDtypeStruct((8, depth), f32))
    if norm == "last":
        in_specs += [whole((8, depth)), whole((8, half)), whole((1, depth))]
        out_specs.append(whole((8, half)))
        out_shape.append(jax.ShapeDtypeStruct((8, half), f32))
        scratch = [pltpu.VMEM((8, depth), f32)]
    flops = 2 * (tokens // 2) * depth * sum(w.shape[1] for w in ws)
    return pl.pallas_call(
        functools.partial(rows_kernel, len(lows), norm),
        grid_spec=pltpu.PrefetchScalarGridSpec(
            num_scalar_prefetch=1,
            grid=(tp // 2,),
            in_specs=in_specs,
            out_specs=tuple(out_specs),
            scratch_shapes=scratch,
        ),
        out_shape=tuple(out_shape),
        compiler_params=params(),
        name="to_rows",
        cost_estimate=cost(flops, 8),
    )(me, *lows, *ws, *extra)


def part_kernel(width, me_ref, own, other, step, out):
    upper = lax.rem(lax.div(me_ref[1], 2), 2) == 1
    both = own[...].astype(f32) + other[...].astype(f32)
    part = jnp.where(upper, pltpu.roll(both, LANES - width, 1), both)
    lane = lax.broadcasted_iota(jnp.int32, part.shape, 1)
    out[...] = jnp.where(lane < width, part, pltpu.roll(step[...].astype(f32), width, 1)).astype(bf16)


def part_call(me, own, other, small_low, width):
    tokens = own.shape[0]
    spec = pl.BlockSpec((tokens // 2, LANES), lambda i: (i, 0))
    last = small_low.shape[1] // LANES - 1
    return pl.pallas_call(
        functools.partial(part_kernel, width),
        grid=(2,),
        in_specs=[smem_spec(), spec, spec, pl.BlockSpec((tokens // 2, LANES), lambda i: (i, last))],
        out_specs=spec,
        out_shape=jax.ShapeDtypeStruct((tokens, LANES), bf16),
        compiler_params=params(),
        name="state_part",
        cost_estimate=cost(0, 1),
    )(me, own, other, small_low)


def rank_of(part, tp):
    bits = tp.bit_length() - 1
    return sum(((part >> b) & 1) << (bits - 1 - b) for b in range(bits))


def state_kernel(tp, width, heads, me_ref, *refs):
    parts, state, step = refs[:tp], refs[tp], refs[tp + 1]
    held = refs[tp + 2]
    for k in range(tp):
        held[k] = parts[k][...]
    lane = lax.broadcasted_iota(jnp.int32, held.shape[1:], 1)
    for j in range(tp * width // LANES):
        low = held[me_ref[1] ^ rank_of(2 * j, tp)]
        high = held[me_ref[1] ^ rank_of(2 * j + 1, tp)]
        state[:, j * LANES : (j + 1) * LANES] = jnp.where(lane < width, low, pltpu.roll(high, width, 1))
    step[...] = pltpu.roll(parts[0][...], LANES - width, 1)[:, :heads]


def state_call(me, parts, tp, width, heads):
    rows = parts[0].shape[0]
    return pl.pallas_call(
        functools.partial(state_kernel, tp, width, heads),
        in_specs=[smem_spec()] + [vmem_spec()] * tp,
        out_specs=(vmem_spec(), vmem_spec()),
        out_shape=(
            jax.ShapeDtypeStruct((rows, tp * width), f32),
            jax.ShapeDtypeStruct((rows, heads), f32),
        ),
        scratch_shapes=[pltpu.VMEM((tp, rows, LANES), f32)],
        compiler_params=params(),
        name="state_grad",
        cost_estimate=cost(0, 1),
    )(me, *parts)


def input_kernel(keep, got, x_ref, cot, gain, out):
    x = x_ref[...]
    inv = lax.rsqrt(jnp.mean(x * x, axis=1, keepdims=True) + norm_eps)
    scaled = (keep[...] + got[...].astype(f32)) * gain[...]
    out[...] = inv * scaled - x * (inv * inv * inv) * jnp.mean(scaled * x, axis=1, keepdims=True) + cot[...]


def input_call(keep, got, x, cot, gain):
    rows, depth = x.shape
    spec = rows_spec(CHUNK // 2, depth)
    return pl.pallas_call(
        input_kernel,
        grid=(2 * rows // CHUNK,),
        in_specs=[spec] * 4 + [full_spec(gain.shape)],
        out_specs=spec,
        out_shape=jax.ShapeDtypeStruct((rows, depth), f32),
        compiler_params=params(),
        name="input_grad",
        cost_estimate=cost(0, 8),
    )(keep, got, x, cot, gain)


def unpack_kernel(count, heads, scols, *refs):
    parts, outs = refs[:count], refs[count:]
    terms = [r[...] for r in parts]
    while len(terms) > 1:
        terms = [terms[i] + terms[i + 1] for i in range(0, len(terms), 2)]
    total = terms[0]
    norm, conv, cbias, sconv, sbias, step_bias, decay, skip, gain = outs
    cols = total.shape[1]
    conv[...] = total[0:4, :]
    cbias[...] = total[4, :]
    for h in range(heads):
        skip[0:1, h : h + 1] = jnp.sum(total[5:6, h * HEADDIM : (h + 1) * HEADDIM], axis=1, keepdims=True)
    row = total[6:7, : cols // 2] + total[6:7, cols // 2 :]
    step_bias[...] = row[:, :heads]
    decay[...] = row[:, LANES : LANES + heads]
    gain[...] = total[7, :]
    norm[pl.ds(0, cols)] = total[8, :]
    norm[pl.ds(cols, cols)] = total[9, :]
    sconv[...] = total[10:14, :scols]
    sbias[...] = total[14, :scols]


def unpack_call(parts, heads, scols, depth):
    cols = parts[0].shape[1]
    shapes = [(depth,), (4, cols), (cols,), (4, scols), (scols,), (1, heads), (1, heads), (1, heads), (cols,)]
    return pl.pallas_call(
        functools.partial(unpack_kernel, len(parts), heads, scols),
        in_specs=[vmem_spec()] * len(parts),
        out_specs=(vmem_spec(),) * len(shapes),
        out_shape=tuple(jax.ShapeDtypeStruct(shape, f32) for shape in shapes),
        compiler_params=params(),
        name="small_grads",
        cost_estimate=cost(0, 1),
    )(*parts)


def causal_taps(buf, conv, bias):
    taps = conv.shape[0]
    held = buf[...]
    total = bias + held[8:, :] * conv[taps - 1 : taps, :]
    for back in range(1, taps):
        total = total + pltpu.roll(held, back, 0)[8:, :] * conv[taps - 1 - back : taps - back, :]
    return total


def conv_back(buf, rows, conv, pre, sums):
    taps = conv.shape[0]
    held = buf[...]
    total = None
    for ahead in range(taps):
        k = taps - 1 - ahead
        part = (pltpu.roll(held, held.shape[0] - ahead, 0) if ahead else held)[:rows, :]
        total = part * conv[k : k + 1, :] + (0.0 if total is None else total)
        sums[k, :, :] += fold(part * pre)
    sums[taps, :, :] += fold(held[:rows, :])
    return total.astype(bf16)


def tri(rows, upper):
    i = lax.broadcasted_iota(jnp.int32, (rows, rows), 0)
    j = lax.broadcasted_iota(jnp.int32, (rows, rows), 1)
    return jnp.where(i <= j if upper else i >= j, 1.0, 0.0).astype(f32)


def small_kernel(tp, ns, table, me_ref, *refs):
    normed_blocks, blocks = refs[:tp], refs[tp : tp + ns]
    conv, cbias, sbias, rate = refs[tp + ns : tp + ns + 4]
    normed, wst, state_pre, u_out, bc, step_v, cum, halo, sems_t, sems_d = refs[tp + ns + 4 :]
    i = pl.program_id(0)
    cols = conv.shape[1]

    @pl.when(i == 0)
    def _():
        wide = wst.shape[1]
        first = blocks[0].shape[1] - wide
        copies = []
        rows = normed.shape[0] // tp
        for k, ref in enumerate(normed_blocks):
            at = pl.multiple_of((me_ref[1] ^ k) * rows, rows)
            copies.append(pltpu.make_async_copy(ref, normed.at[pl.ds(at, rows), :], sems_t.at[k]))
        for c in copies:
            c.start()
        place([([r.at[:, pl.ds(first, wide)] for r in blocks], table, wst, sems_d)], me_ref[0])
        for c in copies:
            c.wait()

    @pl.when(i % (SEQLEN // ROWS) == 0)
    def _():
        halo[0:8, :] = jnp.zeros((8, cols), f32)

    at = pl.multiple_of(i * ROWS, ROWS)
    pre = dot_nn(normed[pl.ds(at, ROWS), :], wst[...])
    state_pre[...] = pre[:, :cols]
    halo[pl.ds(8, ROWS), :] = pre[:, :cols]
    u = causal_taps(halo, conv[...], cbias[...])
    halo[0:8, :] = halo[pl.ds(ROWS, 8), :]
    u_out[...] = u
    bc[...] = (u * sigmoid(u)).astype(bf16)
    v = pre[:, cols:] + sbias[...]
    step_v[...] = v
    a = (jnp.maximum(v, 0.0) + jnp.log1p(jnp.exp(-jnp.abs(v)))) * rate[...]
    low = tri(CHUNK, False)
    for c in range(ROWS // CHUNK):
        part = a[c * CHUNK : (c + 1) * CHUNK, :]
        cum[c * CHUNK : (c + 1) * CHUNK, :] = LOG2E * lax.dot_general(
            low, part, (((1,), (0,)), ((), ())), precision=lax.Precision.HIGHEST, preferred_element_type=f32
        )


def small_call(me, normed_blocks, blocks, conv, cbias, sbias, rate):
    blocks, table = blocks
    tp, ns = len(normed_blocks), len(blocks)
    r, depth = normed_blocks[0].shape
    tokens = tp * r
    cols = conv.shape[1]
    wide = cols + LANES
    out_shape = (
        jax.ShapeDtypeStruct((tokens, depth), bf16),
        jax.ShapeDtypeStruct((depth, wide), bf16),
        jax.ShapeDtypeStruct((tokens, cols), f32),
        jax.ShapeDtypeStruct((tokens, cols), f32),
        jax.ShapeDtypeStruct((tokens, cols), bf16),
        jax.ShapeDtypeStruct((tokens, LANES), f32),
        jax.ShapeDtypeStruct((tokens, LANES), f32),
    )
    return pl.pallas_call(
        functools.partial(small_kernel, tp, ns, table),
        grid=(tokens // ROWS,),
        in_specs=[smem_spec()]
        + [any_spec()] * (tp + ns)
        + [full_spec(conv.shape), full_spec(cbias.shape), full_spec(sbias.shape), full_spec(rate.shape)],
        out_specs=(
            full_spec((tokens, depth)),
            full_spec((depth, wide)),
            rows_spec(ROWS, cols),
            rows_spec(ROWS, cols),
            rows_spec(ROWS, cols),
            rows_spec(ROWS, LANES),
            rows_spec(ROWS, LANES),
        ),
        out_shape=out_shape,
        scratch_shapes=[
            pltpu.VMEM((ROWS + 8, cols), f32),
            pltpu.SemaphoreType.DMA((tp,)),
            pltpu.SemaphoreType.DMA((ns,)),
        ],
        compiler_params=params(),
        name="small_proj",
        cost_estimate=cost(2 * tokens * depth * wide, 8),
    )(me, *normed_blocks, *blocks, conv, cbias, sbias, rate)


def lane_half():
    return lax.broadcasted_iota(jnp.int32, (CHUNK, LANES), 1) < HEADDIM


def column(a, h):
    return jnp.broadcast_to(a[:, h : h + 1], (CHUNK, LANES))


def scan_fwd_kernel(ns, table, me_ref, *refs):
    blocks = refs[:ns]
    normed, conv, cbias, skip, bc, step_v, cum = refs[ns : ns + 7]
    w_a, w_b, value_pre, u_out, y_out, entering, halo, state, x_buf, xe_buf, ends, sems = refs[ns + 7 :]
    i = pl.program_id(0)
    cols = conv.shape[1]
    nstate = bc.shape[1] // 2
    pairs = cols // LANES

    @pl.when(i == 0)
    def _():
        half = cols // 2
        jobs = [
            ([r.at[:, pl.ds(n * half, half)] for r in blocks], table, w, sems.at[n]) for n, w in enumerate((w_a, w_b))
        ]
        place(jobs, me_ref[0])

    @pl.when(i % (SEQLEN // ROWS) == 0)
    def _():
        halo[0:8, :] = jnp.zeros((8, cols), f32)
        state[...] = jnp.zeros_like(state)

    half = cols // 2
    halo[pl.ds(8, ROWS), :half] = dot_nn(normed[...], w_a[...])
    halo[pl.ds(8, ROWS), half:] = dot_nn(normed[...], w_b[...])
    value_pre[...] = halo[pl.ds(8, ROWS), :]
    u = causal_taps(halo, conv[...], cbias[...])
    halo[0:8, :] = halo[pl.ds(ROWS, 8), :]
    u_out[...] = u
    x_buf[...] = u * sigmoid(u)

    first = lane_half()
    ci = lax.broadcasted_iota(jnp.int32, (CHUNK, CHUNK), 0)
    cj = lax.broadcasted_iota(jnp.int32, (CHUNK, CHUNK), 1)

    def chunk(c):
        at = c * CHUNK
        b = bc[pl.ds(at, CHUNK), :nstate]
        cc = bc[pl.ds(at, CHUNK), nstate:]
        bt = b.astype(f32).T.astype(bf16)
        scores = jnp.where(ci >= cj, dot_nt(cc, b), 0.0)
        cumc = cum[pl.ds(at, CHUNK), :]
        cumt = cumc.T
        v = step_v[pl.ds(at, CHUNK), :]
        dt = jnp.maximum(v, 0.0) + jnp.log1p(jnp.exp(-jnp.abs(v)))
        sb = state[...].astype(bf16)
        entering[c] = sb
        y_out[pl.ds(at, CHUNK), :] = dot_nn(cc, sb)
        for g in range(pairs):
            lanes = slice(g * LANES, (g + 1) * LANES)
            c0, c1 = column(cumc, 2 * g), column(cumc, 2 * g + 1)
            m0 = scores * jnp.exp2(jnp.minimum(c0 - cumt[2 * g : 2 * g + 1, :], 0.0))
            m1 = scores * jnp.exp2(jnp.minimum(c1 - cumt[2 * g + 1 : 2 * g + 2, :], 0.0))
            m2 = jnp.concatenate([m0.astype(bf16), m1.astype(bf16)], axis=1)
            cumx = jnp.where(first, c0, c1)
            dtx = jnp.where(first, column(dt, 2 * g), column(dt, 2 * g + 1))
            x = x_buf[pl.ds(at, CHUNK), lanes]
            xs = x * dtx
            xsb = xs.astype(bf16)
            zero = jnp.zeros_like(xsb)
            x2 = jnp.concatenate([jnp.where(first, xsb, zero), jnp.where(first, zero, xsb)], axis=0)
            here = y_out[pl.ds(at, CHUNK), lanes]
            y_out[pl.ds(at, CHUNK), lanes] = dot_nn(m2, x2) + here * jnp.exp2(cumx) + x * skip[:, lanes]
            endx = cumx[CHUNK - 1 : CHUNK, :]
            ends[:, lanes] = jnp.exp2(endx)
            xe_buf[:, lanes] = (xs * jnp.exp2(endx - cumx)).astype(bf16)
        state[...] = state[...] * ends[...] + dot_nn(bt, xe_buf[...])

    for c in range(ROWS // CHUNK):
        chunk(c)


def scan_fwd_call(me, blocks, normed, conv, cbias, skip, bc, step_v, cum):
    blocks, table = blocks
    ns = len(blocks)
    tokens, depth = normed.shape
    cols = conv.shape[1]
    nstate = bc.shape[1] // 2
    chunks = tokens // CHUNK
    per = ROWS // CHUNK
    return pl.pallas_call(
        functools.partial(scan_fwd_kernel, ns, table),
        grid=(tokens // ROWS,),
        in_specs=[smem_spec()]
        + [any_spec()] * ns
        + [
            rows_spec(ROWS, depth),
            full_spec(conv.shape),
            full_spec(cbias.shape),
            full_spec(skip.shape),
            rows_spec(ROWS, 2 * nstate),
            rows_spec(ROWS, LANES),
            rows_spec(ROWS, LANES),
        ],
        out_specs=(
            full_spec((depth, cols // 2)),
            full_spec((depth, cols // 2)),
            rows_spec(ROWS, cols),
            rows_spec(ROWS, cols),
            rows_spec(ROWS, cols),
            pl.BlockSpec((per, nstate, cols), lambda i: (i, 0, 0)),
        ),
        out_shape=(
            jax.ShapeDtypeStruct((depth, cols // 2), bf16),
            jax.ShapeDtypeStruct((depth, cols // 2), bf16),
            jax.ShapeDtypeStruct((tokens, cols), f32),
            jax.ShapeDtypeStruct((tokens, cols), f32),
            jax.ShapeDtypeStruct((tokens, cols), f32),
            jax.ShapeDtypeStruct((chunks, nstate, cols), bf16),
        ),
        scratch_shapes=[
            pltpu.VMEM((ROWS + 8, cols), f32),
            pltpu.VMEM((nstate, cols), f32),
            pltpu.VMEM((ROWS, cols), f32),
            pltpu.VMEM((CHUNK, cols), bf16),
            pltpu.VMEM((1, cols), f32),
            pltpu.SemaphoreType.DMA((2, ns)),
        ],
        compiler_params=params(),
        name="scan_fwd",
        cost_estimate=pl.CostEstimate(
            flops=4 * tokens * depth * cols, bytes_accessed=20 * 1024 * 1024, transcendentals=0
        ),
    )(me, *blocks, normed, conv, cbias, skip, bc, step_v, cum)


def row_form(col):
    parts = []
    for c in range(ROWS // CHUNK):
        wide = jnp.broadcast_to(col[c * CHUNK : (c + 1) * CHUNK, :], (CHUNK, LANES))
        parts.append(wide.T[0:8, :][None])
    return jnp.concatenate(parts, axis=0)


def col_form(rows):
    parts = [jnp.broadcast_to(rows[c, 0:1, :], (CHUNK, LANES)).T for c in range(rows.shape[0])]
    return jnp.concatenate(parts, axis=0)


def widen(tile, cols):
    return jnp.concatenate([tile] * (cols // LANES), axis=1)


def gate_kernel(ns, table, me_ref, *refs):
    blocks = refs[:ns]
    normed, y, w_out, gate_pre, gated_out, squares, sems = refs[ns:]

    @pl.when(pl.program_id(0) == 0)
    def _():
        place([(blocks, table, w_out, sems)], me_ref[0])

    pre = dot_nn(normed[...], w_out[...])
    gate_pre[...] = pre
    gated = y[...] * (pre * sigmoid(pre))
    gated_out[...] = gated
    squares[...] = row_form(jnp.sum(gated * gated, axis=1, keepdims=True))


def stat_spec():
    return pl.BlockSpec((ROWS // CHUNK, 8, LANES), lambda i: (i, 0, 0))


def gate_call(me, blocks, normed, y):
    blocks, table = blocks
    ns = len(blocks)
    tokens, depth = normed.shape
    cols = y.shape[1]
    return pl.pallas_call(
        functools.partial(gate_kernel, ns, table),
        grid=(tokens // ROWS,),
        in_specs=[smem_spec()] + [any_spec()] * ns + [rows_spec(ROWS, depth), rows_spec(ROWS, cols)],
        out_specs=(full_spec((depth, cols)), rows_spec(ROWS, cols), rows_spec(ROWS, cols), stat_spec()),
        out_shape=(
            jax.ShapeDtypeStruct((depth, cols), bf16),
            jax.ShapeDtypeStruct((tokens, cols), f32),
            jax.ShapeDtypeStruct((tokens, cols), f32),
            jax.ShapeDtypeStruct((tokens // CHUNK, 8, LANES), f32),
        ),
        scratch_shapes=[pltpu.SemaphoreType.DMA((ns,))],
        compiler_params=params(),
        name="gate_proj",
        cost_estimate=pl.CostEstimate(
            flops=2 * tokens * depth * cols, bytes_accessed=16 * 1024 * 1024, transcendentals=0
        ),
    )(me, *blocks, normed, y)


def mixed_kernel(inner, nb, me_ref, *refs):
    blocks, stats = refs[:nb], refs[nb : 2 * nb]
    gated, gain, mixed, squares, cot, sems = refs[2 * nb :]

    @pl.when(pl.program_id(0) == 0)
    def _():
        place([(blocks, plain(nb), cot, sems)], me_ref[1])

    total = pair_sum([r[...] for r in stats])
    squares[...] = total
    inv = lax.rsqrt(col_form(total) * (1.0 / inner) + norm_eps)
    mixed[...] = (gated[...] * widen(inv, gated.shape[1]) * gain[...]).astype(bf16)


def mixed_call(me, cot_blocks, gated, stats, gain, inner):
    tokens, cols = gated.shape
    nb = len(cot_blocks)
    depth = cot_blocks[0].shape[1]
    return pl.pallas_call(
        functools.partial(mixed_kernel, inner, nb),
        grid=(tokens // ROWS,),
        in_specs=[smem_spec()]
        + [any_spec()] * nb
        + [stat_spec()] * nb
        + [rows_spec(ROWS, cols), full_spec(gain.shape)],
        out_specs=(rows_spec(ROWS, cols), stat_spec(), full_spec((tokens, depth))),
        out_shape=(
            jax.ShapeDtypeStruct((tokens, cols), bf16),
            jax.ShapeDtypeStruct(stats[0].shape, f32),
            jax.ShapeDtypeStruct((tokens, depth), bf16),
        ),
        scratch_shapes=[pltpu.SemaphoreType.DMA((nb,))],
        compiler_params=params(),
        name="mixed_rows",
        cost_estimate=cost(0, 8),
    )(me, *cot_blocks, *stats, gated, gain)


def out_kernel(ns, table, me_ref, *refs):
    blocks = refs[:ns]
    cot, gated, gain, w_out, mixed_grad, dots, sems = refs[ns:]

    @pl.when(pl.program_id(0) == 0)
    def _():
        place([(blocks, table, w_out, sems)], me_ref[0])

    grad = dot_nn(cot[...], w_out[...])
    mixed_grad[...] = grad
    dots[...] = row_form(jnp.sum(grad * gain[...] * gated[...], axis=1, keepdims=True))


def out_call(me, blocks, cot, gated, gain):
    blocks, table = blocks
    ns = len(blocks)
    tokens, depth = cot.shape
    cols = gated.shape[1]
    return pl.pallas_call(
        functools.partial(out_kernel, ns, table),
        grid=(tokens // ROWS,),
        in_specs=[smem_spec()]
        + [any_spec()] * ns
        + [rows_spec(ROWS, depth), rows_spec(ROWS, cols), full_spec(gain.shape)],
        out_specs=(full_spec((depth, cols)), rows_spec(ROWS, cols), stat_spec()),
        out_shape=(
            jax.ShapeDtypeStruct((depth, cols), bf16),
            jax.ShapeDtypeStruct((tokens, cols), f32),
            jax.ShapeDtypeStruct((tokens // CHUNK, 8, LANES), f32),
        ),
        scratch_shapes=[pltpu.SemaphoreType.DMA((ns,))],
        compiler_params=params(),
        name="mixed_grad",
        cost_estimate=pl.CostEstimate(
            flops=2 * tokens * depth * cols, bytes_accessed=16 * 1024 * 1024, transcendentals=0
        ),
    )(me, *blocks, cot, gated, gain)


def fold(a):
    return a.reshape(a.shape[0] // 8, 8, a.shape[1]).sum(axis=0)


def gated_grad_kernel(inner, nb, *refs):
    stats = refs[:nb]
    mixed_grad, gate_pre, y, squares, gain, gate_low, y_grad, gain_grad = refs[nb:]
    cols = y.shape[1]

    @pl.when(pl.program_id(0) == 0)
    def _():
        gain_grad[...] = jnp.zeros_like(gain_grad)

    inv = lax.rsqrt(col_form(squares[...]) * (1.0 / inner) + norm_eps)
    slope = widen(inv * inv * inv * (col_form(pair_sum([r[...] for r in stats])) * (1.0 / inner)), cols)
    inv = widen(inv, cols)
    pre, ys, grad = gate_pre[...], y[...], mixed_grad[...]
    sig = sigmoid(pre)
    silu = pre * sig
    gated = ys * silu
    grad = grad * inv
    gain_grad[...] += fold(grad * gated)
    gg = grad * gain[...] - gated * slope
    y_grad[...] = gg * silu
    gate_low[...] = (gg * ys * (sig + silu * (1.0 - sig))).astype(bf16)


def gated_grad_call(stats, mixed_grad, gate_pre, y, squares, gain, inner):
    tokens, cols = y.shape
    nb = len(stats)
    big = rows_spec(ROWS, cols)
    return pl.pallas_call(
        functools.partial(gated_grad_kernel, inner, nb),
        grid=(tokens // ROWS,),
        in_specs=[stat_spec()] * nb + [big, big, big, stat_spec(), full_spec(gain.shape)],
        out_specs=(big, big, full_spec((8, cols))),
        out_shape=(
            jax.ShapeDtypeStruct((tokens, cols), bf16),
            jax.ShapeDtypeStruct((tokens, cols), f32),
            jax.ShapeDtypeStruct((8, cols), f32),
        ),
        compiler_params=params(),
        name="gated_grad",
        cost_estimate=cost(0, 14),
    )(*stats, mixed_grad, gate_pre, y, squares, gain)


def scan_bwd_kernel(
    first_head, last, me_ref, y_grad, u_in, value_pre, entering, bc, us, state_pre, step_v, cum, conv, sconv, skip, rate,
    spread, gain_grad, before, *rest,
):
    if last:
        (value_low, small_low, sent, kept, local, state_rows, *rest) = rest
    else:
        (value_low, partial, local, *rest) = rest
    sums_v, sums_s, sums_h, du_buf, ds_buf, carried, bds_buf, yo_buf, xe_buf, dye_buf, lane_buf, ends = rest
    i = pl.program_id(0)
    cols = conv.shape[1]
    scols = sconv.shape[1]
    nstate = scols // 2
    pairs = cols // LANES

    @pl.when(i == 0)
    def _():
        sums_v[...] = jnp.zeros_like(sums_v)
        sums_s[...] = jnp.zeros_like(sums_s)
        sums_h[...] = jnp.zeros_like(sums_h)

    @pl.when(i % (SEQLEN // CHUNK) == 0)
    def _():
        du_buf[pl.ds(CHUNK, 8), :] = jnp.zeros((8, cols), f32)
        ds_buf[pl.ds(CHUNK, 8), :] = jnp.zeros((8, scols), f32)
        carried[...] = jnp.zeros_like(carried)

    first = lane_half()
    ci = lax.broadcasted_iota(jnp.int32, (CHUNK, CHUNK), 0)
    cj = lax.broadcasted_iota(jnp.int32, (CHUNK, CHUNK), 1)

    b = bc[:, :nstate]
    cc = bc[:, nstate:]
    ct = cc.astype(f32).T.astype(bf16)
    scores = jnp.where(ci >= cj, dot_nt(cc, b), 0.0)
    strict = jnp.where(ci > cj, scores, 0.0)
    cumc = cum[...]
    cumt = cumc.T
    v = step_v[...]
    dt = jnp.maximum(v, 0.0) + jnp.log1p(jnp.exp(-jnp.abs(v)))
    dsb = carried[...].astype(bf16)
    sin = entering[0]
    bds_buf[...] = dot_nn(b, dsb)
    yo_buf[...] = dot_nn(cc, sin)

    dscores = jnp.zeros((CHUNK, CHUNK), f32)
    rowacc = jnp.zeros((CHUNK, LANES), f32)
    colsums = []
    for g in range(pairs):
        lanes = slice(g * LANES, (g + 1) * LANES)
        h = first_head + 2 * g
        c0, c1 = column(cumc, h), column(cumc, h + 1)
        d0 = jnp.exp2(jnp.minimum(c0 - cumt[h : h + 1, :], 0.0))
        d1 = jnp.exp2(jnp.minimum(c1 - cumt[h + 1 : h + 2, :], 0.0))
        m2t = jnp.concatenate([scores * d0, scores * d1], axis=1).T.astype(bf16)
        cumx = jnp.where(first, c0, c1)
        endx = cumx[CHUNK - 1 : CHUNK, :]
        toend = jnp.exp2(endx - cumx)
        dtx = jnp.where(first, column(dt, h), column(dt, h + 1))
        u = u_in[:, lanes]
        sig = sigmoid(u)
        x = u * sig
        xs = x * dtx
        xsb = xs.astype(bf16)
        zero = jnp.zeros_like(xsb)
        x2 = jnp.concatenate([jnp.where(first, xsb, zero), jnp.where(first, zero, xsb)], axis=0)
        dy = y_grad[:, lanes]
        dyb = dy.astype(bf16)
        dm = dot_nt(dyb, x2)
        t0 = dm[:, :CHUNK] * d0
        t1 = dm[:, CHUNK:] * d1
        dscores = dscores + (t0 + t1)
        g0 = t0 * strict
        g1 = t1 * strict
        rowacc = jnp.where(cj == h, jnp.sum(g0, axis=1, keepdims=True), rowacc)
        rowacc = jnp.where(cj == h + 1, jnp.sum(g1, axis=1, keepdims=True), rowacc)
        colsums += [jnp.sum(g0, axis=0, keepdims=True), jnp.sum(g1, axis=0, keepdims=True)]
        both = dot_nn(m2t, dyb)
        bds = bds_buf[:, lanes] * toend
        dxs = jnp.where(first, both[:CHUNK, :], both[CHUNK:, :]) + bds
        dye = dy * jnp.exp2(cumx)
        dye_buf[:, lanes] = dye.astype(bf16)
        xe_buf[:, lanes] = (xs * toend).astype(bf16)
        grow = jnp.exp2(endx)
        ends[:, lanes] = grow
        edge = grow * jnp.sum(fold(sin[:, lanes].astype(f32) * carried[:, lanes]), axis=0, keepdims=True)
        lane_buf[pl.ds(0, CHUNK), lanes] = (dye * yo_buf[:, lanes]).astype(bf16)
        lane_buf[pl.ds(CHUNK, CHUNK), lanes] = (xs * bds).astype(bf16)
        lane_buf[pl.ds(2 * CHUNK, CHUNK), lanes] = (dxs * x).astype(bf16)
        lane_buf[pl.ds(3 * CHUNK, 16), lanes] = jnp.broadcast_to(edge, (16, LANES)).astype(bf16)
        sums_v[5, :, lanes] += fold(dy * x)
        du_buf[pl.ds(0, CHUNK), lanes] = (dxs * dtx + dy * skip[:, lanes]) * (sig + x * (1.0 - sig))

    value_low[...] = conv_back(du_buf, CHUNK, conv[...], value_pre[...], sums_v)
    du_buf[pl.ds(CHUNK, 8), :] = du_buf[pl.ds(0, 8), :]

    dscores = jnp.where(ci >= cj, dscores, 0.0)
    db = dot_nt(xe_buf[...], dsb) + dot_nn(dscores.T.astype(bf16), cc)
    dc = dot_nt(dye_buf[...], sin) + dot_nn(dscores.astype(bf16), b)
    carried[...] = carried[...] * ends[...] + dot_nn(ct, dye_buf[...])

    lane_sums = dot_nn(lane_buf[...], spread[...])
    rows = [jnp.zeros((first_head, CHUNK), f32)] if first_head else []
    rows += colsums + [jnp.zeros((LANES - first_head - len(colsums), CHUNK), f32)]
    colt = jnp.concatenate(rows, axis=0).T
    qsum = lane_sums[CHUNK : 2 * CHUNK, :]
    dcum = rowacc - colt + lane_sums[:CHUNK, :] - qsum
    dend = lane_sums[3 * CHUNK : 3 * CHUNK + 1, :] + jnp.sum(fold(qsum), axis=0, keepdims=True)
    dcum = dcum + jnp.where(ci == CHUNK - 1, dend, 0.0)
    da = lax.dot_general(
        tri(CHUNK, True), dcum, (((1,), (0,)), ((), ())), precision=lax.Precision.HIGHEST, preferred_element_type=f32
    )
    ddt = lane_sums[2 * CHUNK : 3 * CHUNK, :] + da * rate[...]
    dv = ddt / (1.0 + jnp.exp(-v))
    sums_h[0, :, :] += fold(dv)
    sums_h[1, :, :] += fold(da * dt) * rate[...]

    done = i == pl.num_programs(0) - 1

    @pl.when(done)
    def _():
        local[...] = jnp.zeros_like(local)
        for k in range(6):
            local[k : k + 1, :] = jnp.sum(sums_v[k], axis=0, keepdims=True)
        for k in range(2):
            local[6:7, k * LANES : (k + 1) * LANES] = jnp.sum(sums_h[k], axis=0, keepdims=True)
        local[7:8, :] = jnp.sum(gain_grad[...], axis=0, keepdims=True)

    dbc = jnp.concatenate([db, dc], axis=1)
    if not last:
        partial[:, :scols] = dbc
        partial[:, scols:] = dv
        return
    if before is not None:
        dbc = dbc + before[:, :scols]
        dv = dv + before[:, scols:]
    uu = us[...]
    sg = sigmoid(uu)
    ds_buf[pl.ds(0, CHUNK), :] = dbc * (sg * (1.0 + uu * (1.0 - sg)))
    low = conv_back(ds_buf, CHUNK, sconv[...], state_pre[...], sums_s)
    ds_buf[pl.ds(CHUNK, 8), :] = ds_buf[pl.ds(0, 8), :]
    small_low[:, :scols] = low
    small_low[:, scols:] = dv.astype(bf16)
    halves = jnp.full((CHUNK, nstate), lax.rem(me_ref[1], 2), jnp.int32) == 0
    kept[...] = jnp.where(halves, low[:, :nstate], low[:, nstate:])
    sent[...] = jnp.where(halves, low[:, nstate:], low[:, :nstate])

    @pl.when(done)
    def _():
        state_rows[...] = jnp.zeros_like(state_rows)
        for k in range(5):
            state_rows[2 + k : 3 + k, :scols] = jnp.sum(sums_s[k], axis=0, keepdims=True)


def scan_bwd_call(
    part, parts, me, y_grad, u, value_pre, entering, bc, us, state_pre, step_v, cum, conv, sconv, skip, rate,
    spread, gain_grad, before,
):
    tokens, all_cols = y_grad.shape
    cols = all_cols // parts
    scols = us.shape[1]
    nstate = scols // 2
    chunks = tokens // CHUNK
    last = part == parts - 1

    def back(width):
        return pl.BlockSpec((CHUNK, width), lambda i: (chunks - 1 - i, 0))

    mine = pl.BlockSpec((CHUNK, cols), lambda i: (chunks - 1 - i, part))

    def lanes_of(a):
        return pl.BlockSpec((a.shape[0], cols), lambda i: (0, part))

    low = (tokens, scols + LANES)
    out_specs = [back(cols)]
    out_shape = [jax.ShapeDtypeStruct((tokens, cols), bf16)]
    if last:
        out_specs += [back(scols + LANES), back(nstate), back(nstate), full_spec((8, cols)), full_spec((8, all_cols))]
        out_shape += [jax.ShapeDtypeStruct(low, bf16)] + [jax.ShapeDtypeStruct((tokens, nstate), bf16)] * 2
        out_shape += [jax.ShapeDtypeStruct((8, cols), f32), jax.ShapeDtypeStruct((8, all_cols), f32)]
    else:
        out_specs += [back(scols + LANES), full_spec((8, cols))]
        out_shape += [jax.ShapeDtypeStruct(low, f32), jax.ShapeDtypeStruct((8, cols), f32)]
    kernel = functools.partial(scan_bwd_kernel, part * cols // HEADDIM, last)
    extra = [] if before is None else [before]
    if before is None:
        inner = kernel
        kernel = lambda *refs: inner(*refs[:16], None, *refs[16:])
    return pl.pallas_call(
        kernel,
        grid=(chunks,),
        in_specs=[
            smem_spec(),
            mine,
            mine,
            mine,
            pl.BlockSpec((1, nstate, cols), lambda i: (chunks - 1 - i, 0, part)),
            back(scols),
            back(scols),
            back(scols),
            back(LANES),
            back(LANES),
            lanes_of(conv),
            full_spec(sconv.shape),
            lanes_of(skip),
            full_spec(rate.shape),
            pl.BlockSpec((cols, LANES), lambda i: (part, 0)),
            lanes_of(gain_grad),
        ]
        + [back(scols + LANES)] * len(extra),
        out_specs=tuple(out_specs),
        out_shape=tuple(out_shape),
        scratch_shapes=[
            pltpu.VMEM((6, 8, cols), f32),
            pltpu.VMEM((5, 8, scols), f32),
            pltpu.VMEM((2, 8, LANES), f32),
            pltpu.VMEM((CHUNK + 8, cols), f32),
            pltpu.VMEM((CHUNK + 8, scols), f32),
            pltpu.VMEM((nstate, cols), f32),
            pltpu.VMEM((CHUNK, cols), f32),
            pltpu.VMEM((CHUNK, cols), f32),
            pltpu.VMEM((CHUNK, cols), bf16),
            pltpu.VMEM((CHUNK, cols), bf16),
            pltpu.VMEM((3 * CHUNK + 16, cols), bf16),
            pltpu.VMEM((1, cols), f32),
        ],
        compiler_params=params(),
        name="scan_bwd",
        cost_estimate=cost(8 * tokens * 1024 * cols, 12),
    )(me, y_grad, u, value_pre, entering, bc, us, state_pre, step_v, cum, conv, sconv, skip, rate, spread, gain_grad, *extra)


def pad_lanes(a):
    return jnp.pad(a, ((0, 0), (0, LANES - a.shape[1])))


def sum_low(a, b):
    return (a.astype(f32) + b.astype(f32)).astype(bf16)


def block(
    block_input,
    cotangent,
    norm_gain,
    gate_proj,
    value_proj,
    state_proj,
    step_proj,
    value_conv,
    value_conv_bias,
    state_conv,
    state_conv_bias,
    step_bias,
    decay_log,
    skip_gain,
    mixer_gain,
    out_proj,
):
    dp, tp = lax.axis_size("dp"), lax.axis_size("tensor")
    t = lax.axis_index("tensor")
    me = jnp.stack([lax.axis_index("dp"), t]).astype(jnp.int32)
    _, depth = block_input.shape
    cols = value_proj.shape[1]
    heads = step_proj.shape[1]
    scols = state_proj.shape[1]
    inner = cols * tp
    width = scols // tp
    t_radix = [2] * (tp.bit_length() - 1)
    t_order = [[1 << b] for b in range(tp.bit_length() - 1)][::-1]
    d_order, d_radix = dp_masks(dp), radices(dp)

    value_block = jnp.concatenate([value_proj, state_proj, pad_lanes(step_proj)], axis=1)
    value_blocks = gather_dp(value_block, d_order)
    normed, cot_low = norm_call(block_input, cotangent, norm_gain[None])
    normed_blocks = gather_relative(normed, "tensor", t_order)
    gate_blocks = gather_dp(gate_proj, d_order)
    out_blocks = gather_dp(out_proj.T, d_order)
    cot_blocks = gather_relative(cot_low, "tensor", t_order)

    rate_row = pad_lanes(-jnp.exp(decay_log)[None])
    lane_head = lax.broadcasted_iota(jnp.int32, (heads, cols), 1) // HEADDIM
    own_head = lane_head == lax.broadcasted_iota(jnp.int32, (heads, cols), 0)
    skip_row = jnp.sum(jnp.where(own_head, skip_gain[:, None], 0.0), axis=0, keepdims=True)
    gain_row = mixer_gain[None]
    spread = (jnp.arange(cols)[:, None] // HEADDIM == jnp.arange(LANES)[None, :]).astype(bf16)
    normed_all, w_small, state_pre, us, bc, step_v, cum = small_call(
        me, normed_blocks, value_blocks, state_conv, state_conv_bias[None], pad_lanes(step_bias[None]), rate_row
    )
    w_value_a, w_value_b, value_pre, u, y, entering = scan_fwd_call(
        me, value_blocks, normed_all, value_conv, value_conv_bias[None], skip_row, bc, step_v, cum
    )
    w_gate, gate_pre, gated, squares = gate_call(me, gate_blocks, normed_all, y)
    mixed_rows, squares, cot_all = mixed_call(me, cot_blocks, gated, exchange(squares, "tensor"), gain_row, inner)

    def to_owner(a, bs):
        sent, kept = tn_call(me, a, bs, dp)
        return finish(me, "dp", 0, d_radix, sent, kept)

    out_terms = to_owner(cot_all, [mixed_rows])
    w_out, mixed_grad, dots = out_call(me, out_blocks, cot_all, gated, gain_row)
    dots = exchange(dots, "tensor")
    (block_sent,) = rows_call(me, False, [mixed_rows], [w_out], tp)
    (block_kept,) = rows_call(me, True, [mixed_rows], [w_out], tp)
    block_terms = finish(me, "tensor", 1, t_radix, block_sent, block_kept)
    gate_low, y_grad, gain_grad = gated_grad_call(dots, mixed_grad, gate_pre, y, squares, gain_row, inner)
    gate_terms = to_owner(normed_all, [gate_low])
    shared = (
        me, y_grad, u, value_pre, entering, bc, us, state_pre, step_v, cum,
        value_conv, state_conv, skip_row, rate_row, spread, gain_grad,
    )
    low_a, before, local_a = scan_bwd_call(0, 2, *shared, None)
    low_b, small_low, state_sent, state_kept, local_b, state_rows = scan_bwd_call(1, 2, *shared, before)
    state_sum = sum_low(state_kept, swap(state_sent, "tensor", 1))
    small_rows = part_call(me, state_sum, swap(state_sum, "tensor", 2), small_low, width)
    value_terms = [to_owner(normed_all, [low_a]), to_owner(normed_all, [low_b])]
    small_grad = total_of([to_owner(normed_all, [small_rows])])
    lows, ws = [gate_low, low_a, low_b, small_low], [w_gate, w_value_a, w_value_b, w_small]
    normed_sent, sums = rows_call(me, False, lows, ws, tp, "first", [normed_all])
    normed_kept, shared = rows_call(me, True, lows, ws, tp, "last", [normed_all, sums, state_rows, norm_gain[None]])
    keep, got = finish(me, "tensor", 1, t_radix, normed_sent, normed_kept)
    input_grad = input_call(keep, got, block_input, cotangent, norm_gain[None])
    state_grad, step_grad = state_call(me, exchange(small_grad, "tensor"), tp, width, heads)
    shared = pair_sum(exchange(shared, "tensor"))
    sums = jnp.concatenate([jnp.concatenate([local_a, local_b], axis=1), shared], axis=0)
    low = 1
    for r in d_radix:
        parts = [sums] + [swap(sums, "dp", m * low) for m in range(1, r)]
        low *= r
        if low < dp:
            sums = pair_sum(parts)
    norm, conv, cbias, sconv, sbias, step_bias_grad, decay, skip, gain = unpack_call(parts, heads, scols, depth)
    return (
        total_of([block_terms], block_input),
        input_grad,
        norm,
        total_of([gate_terms]),
        total_of(value_terms),
        state_grad,
        step_grad,
        conv,
        cbias,
        sconv,
        sbias,
        step_bias_grad[0],
        decay[0],
        skip[0],
        gain,
        total_of([out_terms]).T,
    )


def solution(mesh):
    in_specs = (
        P(("dp", "tensor"), None),
        P(("dp", "tensor"), None),
        P(),
        P("dp", "tensor"),
        P("dp", "tensor"),
        P("dp", None),
        P("dp", "tensor"),
        P(None, "tensor"),
        P("tensor"),
        P(),
        P(),
        P("tensor"),
        P("tensor"),
        P("tensor"),
        P("tensor"),
        P("tensor", "dp"),
    )
    out_specs = (
        P(("dp", "tensor"), None),
        P(("dp", "tensor"), None),
        P(),
        P("dp", "tensor"),
        P("dp", "tensor"),
        P("dp", None),
        P("dp", "tensor"),
        P(None, "tensor"),
        P("tensor"),
        P(),
        P(),
        P("tensor"),
        P("tensor"),
        P("tensor"),
        P("tensor"),
        P("tensor", "dp"),
    )
    return jax.shard_map(block, mesh=mesh, in_specs=in_specs, out_specs=out_specs, check_vma=False)
```
